256 devices in a mesh: tile: 64 (over x, z, core), rep: 4 (over y).
Axes of the slice: x: 4, y: 4, z: 8, core: 2. Of those that a mesh axis runs over, the one named last changes fastest.
Arguments:
- stamps: bfloat16 [625, 262144], P(None, ('tile', 'rep')), may hold values from -6 to 6
- spread_coefficients: bfloat16 [4, 10, 262144], P(None, None, ('tile', 'rep')), may hold values from -2.5 to 2.5
- stamp_ivar: bfloat16 [262144], P(('tile', 'rep')), may hold values from 0.5 to 4
- stamp_ccd: int32 [262144], P(('tile', 'rep')), may hold values from 0 to 3
- psf_bases: bfloat16 [1024, 10, 625], P(('tile', 'rep')), may hold values from -3 to 3
- received_sources: int32 [4, 262144], P(None, ('tile', 'rep')), may hold values from 0 to 255, as said below
- recv_counts: int32 [16384, 4], P(('tile', 'rep')), may hold values from 0 to 4, as said below
Outputs:
- snr: float32 [256, 256], P(('tile', 'rep'))
The draws below stay inside these ranges and needn't reach their ends.
Inputs may be any that keep to these rules, and one draw needn't show every extreme that they name: `received_sources`: entry 0 of a slot is the source the stamp is centred on; the 4 sources of one slot differ. `recv_counts`: in every draw some device receives 4 live slots for one of its blobs from every exposure owner.
All inputs are finite; a program needn't handle non-finite values.
Results may differ from the reference program's by a relative error of at most 0.0032.
Values may be sent and summed in bfloat16 or wider, within the bound.
A program may use at most 64 MiB of HBM per device.

```python
import math
import jax
import jax.numpy as jnp
from jax import lax

SIDE = 25
PIX = 625
BASIS_IMAGES = 10
STAMP_SOURCES = 4
BLOB = 256
BLOBS_PER_TILE = 4
CCD_DEV = 4
GROUP_OWNERS = 64
EXPOSURE_GROUPS = 4
OWNER_BLOB_SLOTS = 4
TOTAL_SLOTS = 262144
CCDS = 1024
RECV_ROWS = 16384
BLOBS = 256


def draw_spread_coefficients(key, part):
    leading_key, remaining_key = jax.random.split(jax.random.fold_in(key, 11))
    central_term = jax.random.uniform(leading_key, (STAMP_SOURCES, 1, TOTAL_SLOTS), jnp.float32, 0.5, 1.5)
    remaining_terms = jnp.clip(0.5 * jax.random.normal(remaining_key, (STAMP_SOURCES, BASIS_IMAGES - 1, TOTAL_SLOTS), jnp.float32), -2.5, 2.5)
    return jnp.concatenate([central_term, remaining_terms], axis=1).astype(jnp.bfloat16)


def draw_psf_bases(key, part):
    rough_key, remaining_key = jax.random.split(jax.random.fold_in(key, 23))
    axis_pos = jnp.arange(SIDE, dtype=jnp.float32) - (SIDE - 1) / 2.0
    radius = axis_pos[:, None] ** 2 + axis_pos[None, :] ** 2
    profile = 0.5 + 1.5 * jnp.exp(-radius / (2.0 * (SIDE / 6.0) ** 2))
    rough = jax.random.uniform(rough_key, (CCDS, 1, PIX), jnp.float32, 0.6, 1.4)
    rest_rows = jnp.clip(jax.random.normal(remaining_key, (CCDS, BASIS_IMAGES - 1, PIX), jnp.float32), -3.0, 3.0)
    core_row = profile.reshape(1, 1, PIX) * rough
    return jnp.concatenate([core_row, rest_rows], axis=1).astype(jnp.bfloat16)


def draw_received_sources(key, part):
    own_key, nearby_key = jax.random.split(jax.random.fold_in(key, 37))
    own_ids = jax.random.randint(own_key, (1, TOTAL_SLOTS), 0, BLOB)
    third_part = (BLOB - 1) // 3
    slot_offsets = jax.random.randint(nearby_key, (STAMP_SOURCES - 1, TOTAL_SLOTS), 0, third_part) + 1 + third_part * jnp.arange(STAMP_SOURCES - 1, dtype=jnp.int32)[:, None]
    return jnp.concatenate([own_ids, (own_ids + slot_offsets) % BLOB], axis=0).astype(jnp.int32)


def draw_recv_counts(key, part):
    count_key, full_key = jax.random.split(jax.random.fold_in(key, 41))
    counts = jax.random.randint(count_key, (RECV_ROWS, BLOBS_PER_TILE), OWNER_BLOB_SLOTS // 4, OWNER_BLOB_SLOTS + 1)
    receivers = RECV_ROWS // GROUP_OWNERS
    chosen = jax.random.randint(full_key, (), 0, receivers * BLOBS_PER_TILE)
    row_device = jnp.arange(RECV_ROWS, dtype=jnp.int32)[:, None] // GROUP_OWNERS
    column_ids = jnp.arange(BLOBS_PER_TILE, dtype=jnp.int32)[None, :]
    filled = row_device * BLOBS_PER_TILE + column_ids == chosen
    return jnp.where(filled, OWNER_BLOB_SLOTS, counts).astype(jnp.int32)


def plant(values, rng, smallest, top_value):
    index_at = [jax.random.randint(jax.random.fold_in(rng, axis), (), 0, length) for axis, length in enumerate(values.shape)]
    main_axis = values.shape.index(max(values.shape))
    next_to = index_at[:main_axis] + [(index_at[main_axis] + 1) % values.shape[main_axis]] + index_at[main_axis + 1:]
    return values.at[tuple(index_at)].set(smallest).at[tuple(next_to)].set(top_value)


def steps_of(stream_key, dims, cuts, low, largest):
    level = 1.0
    for position, shards_of in cuts:
        draws = jax.random.uniform(jax.random.fold_in(jax.random.fold_in(stream_key, 6), position), (shards_of,), jnp.float32, low / len(cuts), largest / len(cuts))
        level = level * jnp.repeat(jnp.exp(draws), dims[position] // shards_of).reshape((-1,) + (1,) * (len(dims) - 1 - position))
    return level


def normal_values(key, shape, deviation, limit, cuts=(), kind=jnp.bfloat16):
    level = steps_of(key, shape, cuts, -0.22, 0.18) if cuts else 1.0
    values = jax.random.normal(key, shape, jnp.float32) * deviation * level
    return jnp.minimum(jnp.maximum(values, -limit), limit).astype(kind)


def setup_inputs(seed: int = 0) -> dict:
    keys = jax.random.split(jax.random.key(seed), 8)
    return {
        "stamps": normal_values(keys[0], (PIX, TOTAL_SLOTS), 1.0, 6.0, ((1, 256),)),
        "spread_coefficients": draw_spread_coefficients(jax.random.fold_in(keys[7], 71), 0),
        "stamp_ivar": jnp.clip(jnp.exp(math.log(4.0) - 2.0794415 * jax.random.uniform(keys[2], (TOTAL_SLOTS,), jnp.float32) ** steps_of(keys[2], (TOTAL_SLOTS,), ((0, 256),), -0.2, 0.2)), 0.5, 4.0).astype(jnp.bfloat16),
        "stamp_ccd": plant(jax.random.randint(keys[3], (TOTAL_SLOTS,), 0, CCD_DEV), jax.random.fold_in(keys[3], 1), 0, CCD_DEV - 1).astype(jnp.int32),
        "psf_bases": draw_psf_bases(jax.random.fold_in(keys[7], 71), 0),
        "received_sources": draw_received_sources(jax.random.fold_in(keys[7], 71), 0),
        "recv_counts": draw_recv_counts(jax.random.fold_in(keys[7], 71), 0),
    }


ridge = 1.0
soft_scale = 4.0
maximal_precision = lax.Precision.HIGHEST

def solve_blobs(gram_set, rhs_set):
    order_size = gram_set.shape[-1]
    identity = jnp.eye(order_size, dtype=jnp.float32)
    factor = jnp.linalg.cholesky(gram_set + ridge * identity)
    inverse = lax.linalg.triangular_solve(factor, jnp.broadcast_to(identity, gram_set.shape), left_side=True, lower=True)
    whitened = jnp.einsum('bij,bj->bi', inverse, rhs_set, precision=maximal_precision)
    fluxes = jnp.einsum('bij,bi->bj', inverse, whitened, precision=maximal_precision)
    spread_profile = lax.optimization_barrier(jnp.sum(inverse * inverse, axis=1))
    return fluxes / jnp.sqrt(spread_profile)

def select_pair(array, tile_partition, blob_vector, blob_axis, tile_axis):
    inner = lax.dynamic_index_in_dim(array, blob_vector, blob_axis, keepdims=False)
    return lax.dynamic_index_in_dim(inner, tile_partition, tile_axis, keepdims=False)

def reference(stamps, spread_coefficients, stamp_ivar, stamp_ccd, psf_bases, received_sources, recv_counts):
    stamp_grid = stamps.reshape(PIX, GROUP_OWNERS, EXPOSURE_GROUPS, GROUP_OWNERS, BLOBS_PER_TILE, OWNER_BLOB_SLOTS)
    coefficient_grid = spread_coefficients.reshape(STAMP_SOURCES, BASIS_IMAGES, GROUP_OWNERS, EXPOSURE_GROUPS, GROUP_OWNERS, BLOBS_PER_TILE, OWNER_BLOB_SLOTS)
    ivar_grid = stamp_ivar.reshape(GROUP_OWNERS, EXPOSURE_GROUPS, GROUP_OWNERS, BLOBS_PER_TILE, OWNER_BLOB_SLOTS)
    ccd_grid = stamp_ccd.reshape(GROUP_OWNERS, EXPOSURE_GROUPS, GROUP_OWNERS, BLOBS_PER_TILE, OWNER_BLOB_SLOTS)
    source_layout = received_sources.reshape(STAMP_SOURCES, GROUP_OWNERS, EXPOSURE_GROUPS, GROUP_OWNERS, BLOBS_PER_TILE, OWNER_BLOB_SLOTS)
    count_grid = recv_counts.reshape(GROUP_OWNERS, EXPOSURE_GROUPS, GROUP_OWNERS, BLOBS_PER_TILE)
    owner_rows = (jnp.arange(GROUP_OWNERS, dtype=jnp.int32)[:, None] * EXPOSURE_GROUPS + jnp.arange(EXPOSURE_GROUPS, dtype=jnp.int32)[None, :]) * CCD_DEV
    slot_pos = jnp.arange(OWNER_BLOB_SLOTS, dtype=jnp.int32)

    def one_blob(index):
        tile_partition = (index // BLOBS_PER_TILE).astype(jnp.int32)
        blob_vector = (index % BLOBS_PER_TILE).astype(jnp.int32)
        observed_blob = select_pair(stamp_grid, tile_partition, blob_vector, 4, 3).reshape(PIX, -1).astype(jnp.float32)
        coefficient_blob = select_pair(coefficient_grid, tile_partition, blob_vector, 5, 4).reshape(STAMP_SOURCES, BASIS_IMAGES, -1).astype(jnp.float32)
        ivar_blob = select_pair(ivar_grid, tile_partition, blob_vector, 3, 2).reshape(-1).astype(jnp.float32)
        ccd_blob = (select_pair(ccd_grid, tile_partition, blob_vector, 3, 2) + owner_rows[:, :, None]).reshape(-1).astype(jnp.int32)
        source_table = jnp.transpose(select_pair(source_layout, tile_partition, blob_vector, 4, 1), (0, 2, 1, 3)).reshape(STAMP_SOURCES, -1)
        counts = jnp.transpose(select_pair(count_grid, tile_partition, blob_vector, 3, 0))
        live_blob = (slot_pos[None, None, :] < counts[:, :, None]).astype(jnp.float32).reshape(-1)
        basis_image = jnp.take(psf_bases, ccd_blob, axis=0).astype(jnp.float32)
        model_images = jnp.einsum('rso,osd->rdo', coefficient_blob, basis_image, precision=maximal_precision).astype(jnp.bfloat16)
        model_images = lax.optimization_barrier(model_images).astype(jnp.float32)
        own_ids = source_table[0]
        stack_sum = jax.ops.segment_sum(observed_blob.T * live_blob[:, None], own_ids, num_segments=BLOB)
        count_sum = jax.ops.segment_sum(live_blob, own_ids, num_segments=BLOB)
        stack_mean = (stack_sum / (1.0 + count_sum[:, None])).astype(jnp.bfloat16)
        stack_mean = lax.optimization_barrier(stack_mean)
        own_mean = jnp.take(stack_mean, own_ids, axis=0).astype(jnp.float32).T
        weights = live_blob * ivar_blob / (1.0 + ivar_blob * (observed_blob - own_mean) ** 2 / soft_scale)
        weighted_pixels = weights[None] * model_images
        pairwise_terms = jnp.einsum('akw,ukw->auw', weighted_pixels, model_images, precision=maximal_precision)
        right_hand_slot = jnp.einsum('cna,na->ca', weighted_pixels, observed_blob, precision=maximal_precision)
        gram_blob = jnp.zeros((BLOB, BLOB), jnp.float32).at[source_table[:, None, :], source_table[None, :, :]].add(pairwise_terms)
        rhs_blob = jnp.zeros((BLOB,), jnp.float32).at[source_table].add(right_hand_slot)
        return solve_blobs(gram_blob[None], rhs_blob[None])[0]
    return lax.map(one_blob, jnp.arange(BLOBS, dtype=jnp.int32))
```

```python
import functools

import jax
import jax.numpy as jnp
from jax import lax
from jax.experimental import pallas as pl
from jax.experimental.pallas import tpu as pltpu
from jax.sharding import PartitionSpec as P

F32 = jnp.float32
BF16 = jnp.bfloat16
I32 = jnp.int32
HIGHEST = lax.Precision.HIGHEST

PIX = 625
LANES = 128
CHUNKS = 5
PADPIX = CHUNKS * LANES
TILES = 64
REPS = 4
SLOTS = 1024
BASIS = 10
QUAD = 4
CCD = 4
GROUP = 16
GROUPS = TILES // GROUP
GSLOTS = GROUP * 16
GK = GROUP * CCD * BASIS
ORDER = 256
HALF = 128
TERMS = 24
PAIRS = [(q, r) for q in range(QUAD) for r in range(q, QUAD)]
VMEM = pl.BlockSpec(memory_space=pltpu.VMEM)


def iota(shape, axis):
    return lax.broadcasted_iota(I32, shape, axis)


def pack_body(st_ref, cf_ref, iv_ref, cd_ref, put):
    meta = jnp.concatenate(
        [
            cf_ref[...].astype(F32),
            iv_ref[...].astype(F32),
            cd_ref[...].astype(F32),
            jnp.zeros((LANES - QUAD * BASIS - 2, SLOTS), F32),
        ],
        axis=0,
    )
    put(0, jnp.transpose(meta).astype(BF16).reshape(TILES, 16, LANES))
    for chunk in (4, 0, 1, 2, 3):
        if chunk < CHUNKS - 1:
            block = st_ref[chunk * LANES : (chunk + 1) * LANES, :].astype(F32)
        else:
            body = st_ref[chunk * LANES : PIX - 1, :].astype(F32)
            last = jnp.broadcast_to(st_ref[PIX - 1 : PIX, :].astype(F32), (16, SLOTS))
            row = iota((16, SLOTS), 0)
            tail = jnp.where(row == 0, last, jnp.where(row == 1, 1.0, 0.0))
            block = jnp.concatenate([body, tail], axis=0)
        put(chunk + 1, jnp.transpose(block).astype(BF16).reshape(TILES, 16, LANES))


def pack_kernel(st_ref, cf_ref, iv_ref, cd_ref, out_ref):
    def put(index, value):
        out_ref[:, index * 16 : (index + 1) * 16, :] = value

    pack_body(st_ref, cf_ref, iv_ref, cd_ref, put)


def fill_hot(key_ref, hot_ref):
    hot_ref[...] = (iota((SLOTS, SLOTS), 0) == key_ref[...]).astype(F32).astype(BF16)


def stack_kernel(got_ref, key_ref, xt_ref, table_ref, hot_ref):
    fill_hot(key_ref, hot_ref)
    for chunk in range(CHUNKS):
        rows = got_ref[:, (chunk + 1) * 16 : (chunk + 2) * 16, :].reshape(SLOTS, LANES)
        turned = jnp.transpose(rows.astype(F32)).astype(BF16)
        xt_ref[chunk * LANES : (chunk + 1) * LANES, :] = turned
        part = lax.dot_general(
            turned, hot_ref[...], (((1,), (1,)), ((), ())), preferred_element_type=F32
        )
        for blob in range(REPS):
            table_ref[blob, chunk * LANES : (chunk + 1) * LANES, :] = part[
                :, blob * ORDER : (blob + 1) * ORDER
            ].astype(BF16)


def mean_kernel(part_ref, mean_ref):
    total = part_ref[0].astype(F32)
    for g in range(1, REPS):
        total = total + part_ref[g].astype(F32)
    count = total[PIX : PIX + 1, :]
    mean_ref[...] = (total / (1.0 + count)).astype(BF16)


def fill_select(meta, select_ref):
    for h in range(GROUPS):
        cols = meta[:, h * GSLOTS : (h + 1) * GSLOTS]
        row = iota((GK, GSLOTS), 0)
        col = iota((GK, GSLOTS), 1)
        image = row % (CCD * BASIS)
        seen = (row // (CCD * BASIS)) == (col // 16)
        ccd = cols[QUAD * BASIS + 1 : QUAD * BASIS + 2, :]
        hit = seen & ((image // BASIS).astype(F32) == ccd)
        spread_row = iota((GK, LANES), 0) % BASIS
        spread_col = iota((GK, LANES), 1)
        for q in range(QUAD):
            spread = (spread_col == spread_row + q * BASIS).astype(F32).astype(BF16)
            laid = jnp.dot(spread, cols.astype(BF16), preferred_element_type=F32)
            select_ref[h, :, q * GSLOTS : (q + 1) * GSLOTS] = jnp.where(hit, laid, 0.0).astype(BF16)


def render(bases_ref, select_ref, model_ref):
    for h in range(GROUPS):
        image = lax.dot_general(
            bases_ref[h * GK : (h + 1) * GK, :],
            select_ref[h],
            (((0,), (0,)), ((), ())),
            preferred_element_type=F32,
        )
        for q in range(QUAD):
            model_ref[q, :, h * GSLOTS : (h + 1) * GSLOTS] = image[
                :, q * GSLOTS : (q + 1) * GSLOTS
            ].astype(BF16)


def accumulate(chunk, xt_ref, own_ref, model_ref, scale_ref, term_ref, rows=16):
    for lane in range(SLOTS // LANES):
        at = slice(lane * LANES, (lane + 1) * LANES)
        quarter = jnp.broadcast_to(scale_ref[0:1, at], (rows, LANES))
        live = jnp.broadcast_to(scale_ref[1:2, at], (rows, LANES))

        def step(i, sums):
            here = pl.ds(pl.multiple_of(i * rows, rows), rows)
            there = pl.ds(pl.multiple_of(chunk * LANES + i * rows, rows), rows)
            x = xt_ref[there, at].astype(F32)
            gap = x - own_ref[here, at]
            weight = live / (1.0 + quarter * (gap * gap))
            m = [model_ref[q, there, at].astype(F32) for q in range(QUAD)]
            wm = [weight * v for v in m]
            new = [wm[q] * m[r] for q, r in PAIRS] + [wm[q] * x for q in range(QUAD)]
            return tuple(s + v for s, v in zip(sums, new))

        sums = lax.fori_loop(
            0,
            LANES // rows,
            step,
            tuple(jnp.zeros((rows, LANES), F32) for _ in range(14)),
        )
        for n, s in enumerate(sums):
            term_ref[n, :, at] += s[0:8] + s[8:16]


def finish_terms(term_ref, src_ref):
    rows = [jnp.sum(term_ref[n], axis=0, keepdims=True) for n in range(14)]
    block = jnp.concatenate(
        rows + [src_ref[...].astype(F32), jnp.zeros((TERMS - 18, SLOTS), F32)], axis=0
    )
    one = block.astype(BF16)
    rest = block - one.astype(F32)
    two = rest.astype(BF16)
    three = (rest - two.astype(F32)).astype(BF16)
    row = iota((SLOTS, SLOTS), 0)
    col = iota((SLOTS, SLOTS), 1)
    home = ((row // 4) % 4) * ORDER + (row // 16) * 4 + row % 4
    move = (home == col).astype(F32).astype(BF16)
    moved = jnp.dot(jnp.concatenate([one, two, three], axis=0).astype(BF16), move, preferred_element_type=F32)
    return moved[0:TERMS] + moved[TERMS : 2 * TERMS] + moved[2 * TERMS : 3 * TERMS]


def terms_kernel(
    got_ref, xt_ref, mean_ref, key_ref, src_ref, bases_ref, out_ref,
    hot_ref, select_ref, model_ref, scale_ref, own_ref, term_ref,
):
    fill_hot(key_ref, hot_ref)
    meta = jnp.transpose(got_ref[:, 0:16, :].reshape(SLOTS, LANES).astype(F32))
    ivar = meta[QUAD * BASIS : QUAD * BASIS + 1, :]
    scale_ref[0:1, :] = ivar * 0.25
    scale_ref[1:2, :] = jnp.where(key_ref[...] >= 0, ivar, 0.0)
    fill_select(meta, select_ref)
    render(bases_ref, select_ref, model_ref)
    term_ref[...] = jnp.zeros_like(term_ref)
    for chunk in range(CHUNKS):
        at = slice(chunk * LANES, (chunk + 1) * LANES)
        means = jnp.concatenate([mean_ref[b, at, :] for b in range(REPS)], axis=1)
        own_ref[...] = jnp.dot(means, hot_ref[...], preferred_element_type=F32)
        accumulate(chunk, xt_ref, own_ref, model_ref, scale_ref, term_ref)
    block = finish_terms(term_ref, src_ref)
    for b in range(REPS):
        out_ref[b] = block[:, b * ORDER : (b + 1) * ORDER]


def invert(mat_ref):
    lane = iota((8, LANES), 1)
    sub = iota((8, LANES), 0)

    def block(i, _):
        top = pl.multiple_of(i * 8, 8)
        panel = mat_ref[pl.ds(top, 8), :]
        for j in range(8):
            factor = jnp.broadcast_to(panel[:, j : j + 1], (8, LANES))
            row = jnp.broadcast_to(panel[j : j + 1, :], (8, LANES))
            pivot = 1.0 / jnp.broadcast_to(factor[j : j + 1, :], (8, LANES))
            row = jnp.where(lane == j, 1.0, row) * pivot
            kept = jnp.where(lane == j, 0.0, panel)
            panel = jnp.where(sub == j, row, kept - factor * row)
        for n in range(16):
            old = mat_ref[n * 8 : (n + 1) * 8, :]
            new = jnp.where(lane < 8, 0.0, old)
            for j in range(8):
                new = new - jnp.broadcast_to(old[:, j : j + 1], (8, LANES)) * jnp.broadcast_to(
                    panel[j : j + 1, :], (8, LANES)
                )
            new = jnp.where(n == i, panel, new)
            mat_ref[n * 8 : (n + 1) * 8, :] = pltpu.roll(new, LANES - 8, 1)
        return 0

    lax.fori_loop(0, 16, block, 0)


def full(a, b):
    return jnp.dot(a, b, preferred_element_type=F32, precision=HIGHEST)


def solve(terms, work_ref):
    slots = terms.shape[1]
    where = iota((ORDER, slots), 0).astype(F32)
    hot = [where == terms[14 + q : 15 + q, :] for q in range(QUAD)]
    gram = jnp.zeros((ORDER, ORDER), F32)
    rhs = jnp.zeros((ORDER, slots), F32)
    for r in range(QUAD):
        mixed = jnp.zeros((ORDER, slots), F32)
        for q in range(QUAD):
            n = PAIRS.index((min(q, r), max(q, r)))
            mixed = jnp.where(hot[q], terms[n : n + 1, :], mixed)
        high = mixed.astype(BF16)
        low = (mixed - high.astype(F32)).astype(BF16)
        side = hot[r].astype(F32).astype(BF16)
        for part in (high, low):
            gram = gram + lax.dot_general(
                part, side, (((1,), (1,)), ((), ())), preferred_element_type=F32
            )
        rhs = jnp.where(hot[r], terms[10 + r : 11 + r, :], rhs)
    rhs = jnp.sum(rhs, axis=1, keepdims=True)
    eye = iota((ORDER, ORDER), 0) == iota((ORDER, ORDER), 1)
    gram = gram + jnp.where(eye, 1.0, 0.0)
    a12 = gram[:HALF, HALF:]
    a21 = gram[HALF:, :HALF]
    a22 = gram[HALF:, HALF:]
    eye = eye[:HALF, :HALF]

    def turn(col):
        return jnp.transpose(jnp.broadcast_to(col, (HALF, HALF)))[0:1, :]

    r1, r2 = rhs[:HALF], rhs[HALF:]
    work_ref[...] = gram[:HALF, :HALF]
    invert(work_ref)
    top = work_ref[...]
    tie = full(a21, top)
    work_ref[...] = a22 - full(tie, a12)
    invert(work_ref)
    low = work_ref[...]
    v = r2 - jnp.sum(tie * turn(r1), axis=1, keepdims=True)
    f2_row = jnp.sum(low * v, axis=0, keepdims=True)
    f2_col = jnp.sum(low * turn(v), axis=1, keepdims=True)
    f1_row = jnp.sum(top * r1, axis=0, keepdims=True) - jnp.sum(tie * f2_col, axis=0, keepdims=True)
    d2 = jnp.sum(jnp.where(eye, low, 0.0), axis=0, keepdims=True)
    d1 = jnp.sum(jnp.where(eye, top, 0.0), axis=0, keepdims=True) + jnp.sum(
        full(low, tie) * tie, axis=0, keepdims=True
    )
    return f1_row / jnp.sqrt(d1), f2_row / jnp.sqrt(d2)


def solve_kernel(part_ref, out_ref, work_ref):
    terms = jnp.concatenate([part_ref[g] for g in range(REPS)], axis=1)
    left, right = solve(terms, work_ref)
    out_ref[:, :HALF] = left
    out_ref[:, HALF:] = right


def call(kernel, outs, scratch=(), **kw):
    return pl.pallas_call(
        kernel,
        out_shape=outs,
        scratch_shapes=list(scratch),
        **kw,
    )


def struct(shape, dtype):
    return jax.ShapeDtypeStruct(shape, dtype)


def local(stamps, coefs, ivar, ccd, bases, sources, counts):
    pos = jnp.arange(4, dtype=I32)
    live = (pos[None, None, :] < counts[:, :, None]).reshape(1, SLOTS)
    blob = (jnp.arange(SLOTS, dtype=I32) // 4 % 4).reshape(1, SLOTS)
    key = jnp.where(live, sources[0:1] + blob * ORDER, -1)

    mine = jnp.pad(bases.reshape(CCD * BASIS, PIX), ((0, 0), (0, PADPIX - PIX)))
    every = lax.all_gather(mine, "tile", axis=0, tiled=True)

    packed = call(pack_kernel, struct((TILES, 96, LANES), BF16))(
        stamps, coefs.reshape(QUAD * BASIS, SLOTS), ivar.reshape(1, SLOTS), ccd.reshape(1, SLOTS)
    )
    got = lax.all_to_all(packed, "tile", split_axis=0, concat_axis=0, tiled=True)
    turned, tables = call(
        stack_kernel,
        (struct((PADPIX, SLOTS), BF16), struct((REPS, PADPIX, ORDER), BF16)),
        [pltpu.VMEM((SLOTS, SLOTS), BF16)],
    )(got, key)
    parts = lax.all_to_all(tables, "rep", split_axis=0, concat_axis=0, tiled=True)
    mean = call(mean_kernel, struct((PADPIX, ORDER), BF16))(parts)
    means = lax.all_to_all(
        jnp.broadcast_to(mean[None], (REPS, PADPIX, ORDER)), "rep", split_axis=0, concat_axis=0, tiled=True
    )
    terms = call(
        terms_kernel,
        struct((REPS, TERMS, ORDER), F32),
        [
            pltpu.VMEM((SLOTS, SLOTS), BF16),
            pltpu.VMEM((GROUPS, GK, QUAD * GSLOTS), BF16),
            pltpu.VMEM((QUAD, PADPIX, SLOTS), BF16),
            pltpu.VMEM((8, SLOTS), F32),
            pltpu.VMEM((LANES, SLOTS), F32),
            pltpu.VMEM((14, 8, SLOTS), F32),
        ],
    )(got, turned, means, key, sources, every)
    mixed = lax.all_to_all(terms, "rep", split_axis=0, concat_axis=0, tiled=True)
    return call(solve_kernel, struct((1, ORDER), F32), [pltpu.VMEM((HALF, HALF), F32)])(mixed)


def solution(mesh):
    return jax.shard_map(
        local,
        mesh=mesh,
        in_specs=(
            P(None, ("tile", "rep")),
            P(None, None, ("tile", "rep")),
            P(("tile", "rep")),
            P(("tile", "rep")),
            P(("tile", "rep"), None, None),
            P(None, ("tile", "rep")),
            P(("tile", "rep"), None),
        ),
        out_specs=P(("tile", "rep"), None),
        check_vma=False,
    )
```

```python
import functools

import jax
import jax.numpy as jnp
from jax import lax
from jax.experimental import pallas as pl
from jax.experimental.pallas import tpu as pltpu
from jax.sharding import PartitionSpec as P

F32 = jnp.float32
BF16 = jnp.bfloat16
I32 = jnp.int32
HIGHEST = lax.Precision.HIGHEST

PIX = 625
LANES = 128
CHUNKS = 5
PADPIX = CHUNKS * LANES
TILES = 64
REPS = 4
SLOTS = 1024
BASIS = 10
QUAD = 4
CCD = 4
GROUP = 16
GROUPS = TILES // GROUP
GSLOTS = GROUP * 16
ROWS = 48
GK = GROUP * ROWS
ORDER = 256
HALF = 128
TERMS = 24
PAIRS = [(q, r) for q in range(QUAD) for r in range(q, QUAD)]
MESH = pl.DeviceIdType.MESH
VMEM = pl.BlockSpec(memory_space=pltpu.VMEM)


def iota(shape, axis):
    return lax.broadcasted_iota(I32, shape, axis)


def pack_body(st_ref, cf_ref, iv_ref, cd_ref, put, which):
    if 0 in which:
        meta = jnp.concatenate(
            [
                cf_ref[...].astype(F32),
                iv_ref[...].astype(F32),
                cd_ref[...].astype(F32),
                jnp.zeros((LANES - QUAD * BASIS - 2, SLOTS), F32),
            ],
            axis=0,
        )
        put(0, jnp.transpose(meta).astype(BF16).reshape(TILES, 16, LANES))
    for chunk in range(CHUNKS):
        if chunk + 1 not in which:
            continue
        if chunk < CHUNKS - 1:
            block = st_ref[chunk * LANES : (chunk + 1) * LANES, :].astype(F32)
        else:
            body = st_ref[chunk * LANES : PIX - 1, :].astype(F32)
            last = jnp.broadcast_to(st_ref[PIX - 1 : PIX, :].astype(F32), (16, SLOTS))
            row = iota((16, SLOTS), 0)
            tail = jnp.where(row == 0, last, jnp.where(row == 1, 1.0, 0.0))
            block = jnp.concatenate([body, tail], axis=0)
        put(chunk + 1, jnp.transpose(block).astype(BF16).reshape(TILES, 16, LANES))


def fill_hot(key_ref, hot_ref):
    hot_ref[...] = (iota((SLOTS, SLOTS), 0) == key_ref[...]).astype(F32).astype(BF16)


def fill_select(meta, select_ref):
    for h in range(GROUPS):
        cols = meta[:, h * GSLOTS : (h + 1) * GSLOTS]
        row = iota((GK, GSLOTS), 0)
        col = iota((GK, GSLOTS), 1)
        image = row % ROWS
        seen = (row // ROWS) == (col // 16)
        ccd = cols[QUAD * BASIS + 1 : QUAD * BASIS + 2, :]
        hit = seen & ((image // BASIS).astype(F32) == ccd)
        spread_row = (iota((GK, LANES), 0) % ROWS) % BASIS
        spread_col = iota((GK, LANES), 1)
        for q in range(QUAD):
            spread = (spread_col == spread_row + q * BASIS).astype(F32).astype(BF16)
            laid = jnp.dot(spread, cols.astype(BF16), preferred_element_type=F32)
            select_ref[h, :, q * GSLOTS : (q + 1) * GSLOTS] = jnp.where(hit, laid, 0.0).astype(BF16)


def render(every_ref, select_ref, model_ref):
    for h in range(GROUPS):
        image = lax.dot_general(
            every_ref[h * 8 : (h + 1) * 8].reshape(GK, PADPIX),
            select_ref[h],
            (((0,), (0,)), ((), ())),
            preferred_element_type=F32,
        )
        for q in range(QUAD):
            model_ref[q, :, h * GSLOTS : (h + 1) * GSLOTS] = image[
                :, q * GSLOTS : (q + 1) * GSLOTS
            ].astype(BF16)


def accumulate(chunk, xt_ref, own_ref, model_ref, scale_ref, term_ref, rows=16):
    for lane in range(SLOTS // LANES):
        at = slice(lane * LANES, (lane + 1) * LANES)
        quarter = jnp.broadcast_to(scale_ref[0:1, at], (rows, LANES))
        live = jnp.broadcast_to(scale_ref[1:2, at], (rows, LANES))

        def step(i, sums):
            here = pl.ds(pl.multiple_of(i * rows, rows), rows)
            there = pl.ds(pl.multiple_of(chunk * LANES + i * rows, rows), rows)
            x = xt_ref[there, at].astype(F32)
            gap = x - own_ref[here, at]
            weight = live / (1.0 + quarter * (gap * gap))
            m = [model_ref[q, there, at].astype(F32) for q in range(QUAD)]
            wm = [weight * v for v in m]
            new = [wm[q] * m[r] for q, r in PAIRS] + [wm[q] * x for q in range(QUAD)]
            return tuple(s + v for s, v in zip(sums, new))

        sums = lax.fori_loop(
            0,
            LANES // rows,
            step,
            tuple(jnp.zeros((rows, LANES), F32) for _ in range(14)),
        )
        for n, s in enumerate(sums):
            term_ref[n, :, at] += s[0:8] + s[8:16]


def finish_terms(term_ref, src_ref):
    rows = [jnp.sum(term_ref[n], axis=0, keepdims=True) for n in range(14)]
    block = jnp.concatenate(
        rows + [src_ref[...].astype(F32), jnp.zeros((TERMS - 18, SLOTS), F32)], axis=0
    )
    one = block.astype(BF16)
    rest = block - one.astype(F32)
    two = rest.astype(BF16)
    three = (rest - two.astype(F32)).astype(BF16)
    row = iota((SLOTS, SLOTS), 0)
    col = iota((SLOTS, SLOTS), 1)
    home = ((row // 4) % 4) * ORDER + (row // 16) * 4 + row % 4
    move = (home == col).astype(F32).astype(BF16)
    moved = jnp.dot(jnp.concatenate([one, two, three], axis=0).astype(BF16), move, preferred_element_type=F32)
    return moved[0:TERMS] + moved[TERMS : 2 * TERMS] + moved[2 * TERMS : 3 * TERMS]


def invert(mat_ref):
    lane = iota((8, LANES), 1)
    sub = iota((8, LANES), 0)

    def block(i, _):
        top = pl.multiple_of(i * 8, 8)
        panel = mat_ref[pl.ds(top, 8), :]
        for j in range(8):
            factor = jnp.broadcast_to(panel[:, j : j + 1], (8, LANES))
            row = jnp.broadcast_to(panel[j : j + 1, :], (8, LANES))
            pivot = 1.0 / jnp.broadcast_to(factor[j : j + 1, :], (8, LANES))
            row = jnp.where(lane == j, 1.0, row) * pivot
            kept = jnp.where(lane == j, 0.0, panel)
            panel = jnp.where(sub == j, row, kept - factor * row)
        for n in range(16):
            old = mat_ref[n * 8 : (n + 1) * 8, :]
            new = jnp.where(lane < 8, 0.0, old)
            for j in range(8):
                new = new - jnp.broadcast_to(old[:, j : j + 1], (8, LANES)) * jnp.broadcast_to(
                    panel[j : j + 1, :], (8, LANES)
                )
            new = jnp.where(n == i, panel, new)
            mat_ref[n * 8 : (n + 1) * 8, :] = pltpu.roll(new, LANES - 8, 1)
        return 0

    lax.fori_loop(0, 16, block, 0)


def full(a, b):
    return jnp.dot(a, b, preferred_element_type=F32, precision=HIGHEST)


def solve(terms, work_ref):
    slots = terms.shape[1]
    where = iota((ORDER, slots), 0).astype(F32)
    hot = [where == terms[14 + q : 15 + q, :] for q in range(QUAD)]
    gram = jnp.zeros((ORDER, ORDER), F32)
    rhs = jnp.zeros((ORDER, slots), F32)
    for r in range(QUAD):
        mixed = jnp.zeros((ORDER, slots), F32)
        for q in range(QUAD):
            n = PAIRS.index((min(q, r), max(q, r)))
            mixed = jnp.where(hot[q], terms[n : n + 1, :], mixed)
        high = mixed.astype(BF16)
        low = (mixed - high.astype(F32)).astype(BF16)
        side = hot[r].astype(F32).astype(BF16)
        for part in (high, low):
            gram = gram + lax.dot_general(
                part, side, (((1,), (1,)), ((), ())), preferred_element_type=F32
            )
        rhs = jnp.where(hot[r], terms[10 + r : 11 + r, :], rhs)
    rhs = jnp.sum(rhs, axis=1, keepdims=True)
    eye = iota((ORDER, ORDER), 0) == iota((ORDER, ORDER), 1)
    gram = gram + jnp.where(eye, 1.0, 0.0)
    a12 = gram[:HALF, HALF:]
    a21 = gram[HALF:, :HALF]
    a22 = gram[HALF:, HALF:]
    eye = eye[:HALF, :HALF]

    def turn(col):
        return jnp.transpose(jnp.broadcast_to(col, (HALF, HALF)))[0:1, :]

    r1, r2 = rhs[:HALF], rhs[HALF:]
    work_ref[...] = gram[:HALF, :HALF]
    invert(work_ref)
    top = work_ref[...]
    tie = full(a21, top)
    work_ref[...] = a22 - full(tie, a12)
    invert(work_ref)
    low = work_ref[...]
    v = r2 - jnp.sum(tie * turn(r1), axis=1, keepdims=True)
    f2_row = jnp.sum(low * v, axis=0, keepdims=True)
    f2_col = jnp.sum(low * turn(v), axis=1, keepdims=True)
    f1_row = jnp.sum(top * r1, axis=0, keepdims=True) - jnp.sum(tie * f2_col, axis=0, keepdims=True)
    d2 = jnp.sum(jnp.where(eye, low, 0.0), axis=0, keepdims=True)
    d1 = jnp.sum(jnp.where(eye, top, 0.0), axis=0, keepdims=True) + jnp.sum(
        full(low, tie) * tie, axis=0, keepdims=True
    )
    return f1_row / jnp.sqrt(d1), f2_row / jnp.sqrt(d2)


def remote(src, dst, send, recv, **where):
    return pltpu.make_async_remote_copy(
        src_ref=src, dst_ref=dst, send_sem=send, recv_sem=recv, device_id=where, device_id_type=MESH
    )


def whole_kernel(
    st_ref, cf_ref, iv_ref, cd_ref, key_ref, src_ref, mine_ref, out_ref,
    packed, got, every, xt_ref, hot_ref, select_ref, model_ref, scale_ref, own_ref, term_ref,
    tables, parts, mean_own, means, count_ref, terms_out, terms_in, work_ref,
    a_send, a_recv, b_send, b_recv, t_send, t_recv, m_send, m_recv, e_send, e_recv,
):
    me = lax.axis_index("tile")
    g = lax.axis_index("rep")
    x, z, c = me // 16, (me // 2) % 8, me % 2

    def peer(dx, dz, core):
        return (((x + dx + 4) % 4) * 8 + (z + dz + 8) % 8) * 2 + core

    barrier = pltpu.get_barrier_semaphore()

    def greet(o, _):
        pl.semaphore_signal(barrier, inc=1, device_id={"tile": (me + o) % TILES}, device_id_type=MESH)
        return 0

    lax.fori_loop(1, TILES, greet, 0)
    for d in range(1, REPS):
        pl.semaphore_signal(barrier, inc=1, device_id={"rep": (g + d) % REPS}, device_id_type=MESH)

    def send_block(n):
        def one(o, _):
            p = (me + o) % TILES
            remote(packed.at[n, p], got.at[n, me], a_send.at[n], a_recv.at[n], tile=p).start()
            return 0

        lax.fori_loop(1, TILES, one, 0)
        got[n, pl.ds(me, 1)] = packed[n, pl.ds(me, 1)]

    def block_done(n):
        many = pl.ds(0, TILES - 1)
        return remote(packed.at[n, many], got.at[n, many], a_send.at[n], a_recv.at[n], tile=peer(0, 1, c))

    def blocks_done(stage, count):
        many = every.at[pl.ds(0, count), 0]
        return remote(many, many, b_send.at[stage], b_recv.at[stage], tile=peer(0, 1, c))

    def send_bases(stage, ref, dx, dz, core):
        remote(ref, ref, b_send.at[stage], b_recv.at[stage], tile=peer(dx, dz, core)).start()

    here = x * 8 + z

    def pack(n):
        def put(index, value):
            packed[index] = value

        pack_body(st_ref, cf_ref, iv_ref, cd_ref, put, (n,))

    def stage_z1():
        for dz in (1, -1, 2, -2):
            remote(
                mine_ref, every.at[here, c], b_send.at[0], b_recv.at[0], tile=peer(0, dz, c)
            ).start()

    def stage_z2():
        blocks_done(0, 4).wait_recv()
        low = every.at[x * 8 + (z + 6) % 8, c]
        high = every.at[x * 8 + (z + 2) % 8, c]
        send_bases(1, low, 0, 1, c)
        send_bases(1, high, 0, -1, c)
        send_bases(1, low, 0, 2, c)

    def stage_x1():
        blocks_done(1, 3).wait_recv()
        column = every.at[pl.ds(x * 8, 8), c]
        send_bases(2, column, 1, 0, c)
        send_bases(2, column, -1, 0, c)

    def stage_x2():
        blocks_done(2, 16).wait_recv()
        send_bases(3, every.at[pl.ds(((x + 3) % 4) * 8, 4), c], 1, 0, c)
        send_bases(3, every.at[pl.ds(((x + 1) % 4) * 8 + 4, 4), c], -1, 0, c)

    def stage_core():
        blocks_done(3, 8).wait_recv()
        send_bases(4, every.at[pl.ds(0, 32), c], 0, 0, 1 - c)

    def stack(n):
        block_done(n + 1).wait_recv()
        turned = jnp.transpose(got[n + 1].reshape(SLOTS, LANES).astype(F32)).astype(BF16)
        xt_ref[n * LANES : (n + 1) * LANES, :] = turned
        part = lax.dot_general(
            turned, hot_ref[...], (((1,), (1,)), ((), ())), preferred_element_type=F32
        )
        for b in range(REPS):
            tables[n, b] = part[:, b * ORDER : (b + 1) * ORDER].astype(BF16)
        for d in range(1, REPS):
            b = (g + d) % REPS
            remote(tables.at[n, b], parts.at[n, g], t_send.at[n], t_recv.at[n], rep=b).start()
        parts[n, pl.ds(g, 1)] = tables[n, pl.ds(g, 1)]

    def three(src, dst, send, recv, n):
        many = pl.ds(0, REPS - 1)
        return remote(src.at[n, many], dst.at[n, many], send.at[n], recv.at[n], rep=(g + 1) % REPS)

    def mean(n):
        three(tables, parts, t_send, t_recv, n).wait_recv()
        total = parts[n, 0].astype(F32)
        for other in range(1, REPS):
            total = total + parts[n, other].astype(F32)
        if n == CHUNKS - 1:
            at = PIX - (CHUNKS - 1) * LANES
            count_ref[...] = jnp.broadcast_to(total[at : at + 1, :], (8, ORDER))
        value = (total / (1.0 + count_ref[0:1, :])).astype(BF16)
        mean_own[n, 0] = value
        for d in range(1, REPS):
            remote(
                mean_own.at[n, 0], means.at[n, g], m_send.at[n], m_recv.at[n], rep=(g + d) % REPS
            ).start()
        means[n, pl.ds(g, 1)] = mean_own[n]

    def terms(n):
        three(means, means, m_send, m_recv, n).wait_recv()
        joined = jnp.concatenate([means[n, b] for b in range(REPS)], axis=1)
        own_ref[...] = jnp.dot(joined, hot_ref[...], preferred_element_type=F32)
        accumulate(n, xt_ref, own_ref, model_ref, scale_ref, term_ref)

    pack(0)
    pack(5)
    every[pl.ds(here, 1), pl.ds(c, 1)] = mine_ref[...].reshape(1, 1, ROWS, PADPIX)
    pl.semaphore_wait(barrier, TILES - 1 + REPS - 1)
    stage_z1()
    send_block(0)
    send_block(5)
    pack(1)
    send_block(1)
    stage_z2()
    pack(2)
    send_block(2)
    fill_hot(key_ref, hot_ref)
    term_ref[...] = jnp.zeros_like(term_ref)
    stage_x1()
    pack(3)
    send_block(3)
    block_done(0).wait_recv()
    meta = jnp.transpose(got[0].reshape(SLOTS, LANES).astype(F32))
    ivar = meta[QUAD * BASIS : QUAD * BASIS + 1, :]
    scale_ref[0:1, :] = ivar * 0.25
    scale_ref[1:2, :] = jnp.where(key_ref[...] >= 0, ivar, 0.0)
    stage_x2()
    pack(4)
    send_block(4)
    fill_select(meta, select_ref)
    stack(4)
    stage_core()
    stack(0)
    mean(4)
    stack(1)
    mean(0)
    blocks_done(4, 32).wait_recv()
    render(every, select_ref, model_ref)
    terms(4)
    stack(2)
    mean(1)
    terms(0)
    stack(3)
    mean(2)
    terms(1)
    mean(3)
    terms(2)
    terms(3)
    block = finish_terms(term_ref, src_ref)
    for b in range(REPS):
        terms_out[0, b] = block[:, b * ORDER : (b + 1) * ORDER]
    for d in range(1, REPS):
        b = (g + d) % REPS
        remote(terms_out.at[0, b], terms_in.at[0, g], e_send.at[0], e_recv.at[0], rep=b).start()
    terms_in[0, pl.ds(g, 1)] = terms_out[0, pl.ds(g, 1)]
    three(terms_out, terms_in, e_send, e_recv, 0).wait_recv()
    left, right = solve(jnp.concatenate([terms_in[0, k] for k in range(REPS)], axis=1), work_ref)
    out_ref[:, :HALF] = left
    out_ref[:, HALF:] = right

    for n in range(CHUNKS + 1):
        block_done(n).wait_send()
    for stage, count in enumerate((4, 3, 16, 8, 32)):
        blocks_done(stage, count).wait_send()
    for n in range(CHUNKS):
        three(tables, parts, t_send, t_recv, n).wait_send()
        three(means, means, m_send, m_recv, n).wait_send()
    three(terms_out, terms_in, e_send, e_recv, 0).wait_send()


def struct(shape, dtype):
    return jax.ShapeDtypeStruct(shape, dtype)


def local(stamps, coefs, ivar, ccd, bases, sources, counts):
    pos = jnp.arange(4, dtype=I32)
    live = (pos[None, None, :] < counts[:, :, None]).reshape(1, SLOTS)
    blob = (jnp.arange(SLOTS, dtype=I32) // 4 % 4).reshape(1, SLOTS)
    key = jnp.where(live, sources[0:1] + blob * ORDER, -1)
    mine = jnp.pad(
        bases.reshape(CCD * BASIS, PIX), ((0, ROWS - CCD * BASIS), (0, PADPIX - PIX))
    )
    dma = pltpu.SemaphoreType.DMA
    return pl.pallas_call(
        whole_kernel,
        out_shape=struct((1, ORDER), F32),
        in_specs=[VMEM] * 7,
        out_specs=VMEM,
        scratch_shapes=[
            pltpu.VMEM((CHUNKS + 1, TILES, 16, LANES), BF16),
            pltpu.VMEM((CHUNKS + 1, TILES, 16, LANES), BF16),
            pltpu.VMEM((32, 2, ROWS, PADPIX), BF16),
            pltpu.VMEM((PADPIX, SLOTS), BF16),
            pltpu.VMEM((SLOTS, SLOTS), BF16),
            pltpu.VMEM((GROUPS, GK, QUAD * GSLOTS), BF16),
            pltpu.VMEM((QUAD, PADPIX, SLOTS), BF16),
            pltpu.VMEM((8, SLOTS), F32),
            pltpu.VMEM((LANES, SLOTS), F32),
            pltpu.VMEM((14, 8, SLOTS), F32),
            pltpu.VMEM((CHUNKS, REPS, LANES, ORDER), BF16),
            pltpu.VMEM((CHUNKS, REPS, LANES, ORDER), BF16),
            pltpu.VMEM((CHUNKS, 1, LANES, ORDER), BF16),
            pltpu.VMEM((CHUNKS, REPS, LANES, ORDER), BF16),
            pltpu.VMEM((8, ORDER), F32),
            pltpu.VMEM((1, REPS, TERMS, ORDER), F32),
            pltpu.VMEM((1, REPS, TERMS, ORDER), F32),
            pltpu.VMEM((HALF, HALF), F32),
            dma((CHUNKS + 1,)),
            dma((CHUNKS + 1,)),
            dma((5,)),
            dma((5,)),
            dma((CHUNKS,)),
            dma((CHUNKS,)),
            dma((CHUNKS,)),
            dma((CHUNKS,)),
            dma((1,)),
            dma((1,)),
        ],
        compiler_params=pltpu.CompilerParams(
            collective_id=0, has_side_effects=True, vmem_limit_bytes=60 * 1024 * 1024
        ),
    )(
        stamps,
        coefs.reshape(QUAD * BASIS, SLOTS),
        ivar.reshape(1, SLOTS),
        ccd.reshape(1, SLOTS),
        key,
        sources,
        mine,
    )


def solution(mesh):
    return jax.shard_map(
        local,
        mesh=mesh,
        in_specs=(
            P(None, ("tile", "rep")),
            P(None, None, ("tile", "rep")),
            P(("tile", "rep")),
            P(("tile", "rep")),
            P(("tile", "rep"), None, None),
            P(None, ("tile", "rep")),
            P(("tile", "rep"), None),
        ),
        out_specs=P(("tile", "rep"), None),
        check_vma=False,
    )
```

```python
import functools

import jax
import jax.numpy as jnp
from jax import lax
from jax.experimental import pallas as pl
from jax.experimental.pallas import tpu as pltpu
from jax.sharding import PartitionSpec as P

F32 = jnp.float32
BF16 = jnp.bfloat16
I32 = jnp.int32
HIGHEST = lax.Precision.HIGHEST

PIX = 625
LANES = 128
CHUNKS = 5
PADPIX = CHUNKS * LANES
TILES = 64
REPS = 4
SLOTS = 1024
BASIS = 10
QUAD = 4
CCD = 4
GROUP = 16
GROUPS = TILES // GROUP
GSLOTS = GROUP * 16
ROWS = 48
GK = GROUP * ROWS
ORDER = 256
HALF = 128
TERMS = 16
UNROLL = 2
PAIRS = [(q, r) for q in range(QUAD) for r in range(q, QUAD)]
MESH = pl.DeviceIdType.MESH
VMEM = pl.BlockSpec(memory_space=pltpu.VMEM)


def iota(shape, axis):
    return lax.broadcasted_iota(I32, shape, axis)


def flat(ref):
    return jnp.concatenate([ref[i : i + 1, :].astype(F32) for i in range(8)], axis=1)


def pack_meta(cf_ref, iv_ref, cd_ref, out_ref):
    meta = jnp.concatenate(
        [cf_ref[k].astype(F32) for k in range(BASIS)]
        + [flat(iv_ref), flat(cd_ref), jnp.zeros((LANES - QUAD * BASIS - 2, SLOTS), F32)],
        axis=0,
    )
    rows = jnp.transpose(meta).reshape(TILES, 16, LANES)
    left = rows[:, :8].reshape(TILES * 8, LANES)
    right = rows[:, 8:].reshape(TILES * 8, LANES)
    out_ref[...] = (left + pltpu.roll(right, 64, 1)).reshape(TILES, 8, LANES).astype(BF16)


def unpack_meta(got_ref):
    rows = got_ref[...].astype(F32)
    other = pltpu.roll(rows.reshape(TILES * 8, LANES), 64, 1).reshape(TILES, 8, LANES)
    return jnp.transpose(jnp.concatenate([rows, other], axis=1).reshape(SLOTS, LANES))


def pack_block(st_ref, chunk, out_ref):
    if chunk < CHUNKS - 1:
        block = st_ref[chunk * LANES : (chunk + 1) * LANES, :].astype(F32)
    else:
        body = st_ref[chunk * LANES : PIX - 1, :].astype(F32)
        last = jnp.broadcast_to(st_ref[PIX - 1 : PIX, :].astype(F32), (16, SLOTS))
        row = iota((16, SLOTS), 0)
        tail = jnp.where(row == 0, last, jnp.where(row == 1, 1.0, 0.0))
        block = jnp.concatenate([body, tail], axis=0)
    out_ref[chunk] = jnp.transpose(block).astype(BF16).reshape(TILES, 16, LANES)


def fill_key(counts_ref, src_ref, key_ref):
    owner = (iota((TILES, SLOTS), 0) == iota((TILES, SLOTS), 1) // 16).astype(F32).astype(BF16)
    count = jnp.concatenate(
        [counts_ref[...].astype(F32), jnp.zeros((12, TILES), F32)], axis=0
    ).astype(BF16)
    laid = jnp.dot(count, owner, preferred_element_type=F32)
    lane = iota((1, SLOTS), 1)
    blob = (lane // 4) % 4
    mine = jnp.zeros((1, SLOTS), F32)
    for b in range(REPS):
        mine = jnp.where(blob == b, laid[b : b + 1, :], mine)
    live = (lane % 4).astype(F32) < mine
    key_ref[...] = jnp.where(live, src_ref[0:1, :] + blob * ORDER, -1)


def fill_move(move_ref):
    row = iota((SLOTS, 1), 0)
    home = ((row // 4) % 4) * ORDER + (row // 16) * 4 + row % 4
    move_ref[...] = (home == iota((SLOTS, SLOTS), 1)).astype(F32).astype(BF16)


def fill_hot(key_ref, hot_ref):
    hot_ref[...] = (iota((SLOTS, SLOTS), 0) == key_ref[...]).astype(F32).astype(BF16)


def fill_select(meta, select_ref):
    cols = meta.astype(BF16)
    image = iota((GK, 1), 0) % ROWS
    owner = iota((GK, 1), 0) // ROWS
    own_ccd = jnp.where(image < CCD * BASIS, image % CCD, -1).astype(F32)
    seen = owner == iota((GK, GSLOTS), 1) // 16
    for h in range(GROUPS):
        at = slice(h * GSLOTS, (h + 1) * GSLOTS)
        hit = seen & (own_ccd == meta[QUAD * BASIS + 1 : QUAD * BASIS + 2, at])
        for q in range(QUAD):
            spread = (iota((GK, LANES), 1) == (image // CCD) * QUAD + q).astype(F32).astype(BF16)
            laid = jnp.dot(spread, cols[:, at], preferred_element_type=F32)
            select_ref[h, :, q * GSLOTS : (q + 1) * GSLOTS] = jnp.where(hit, laid, 0.0).astype(BF16)


def render(every_ref, select_ref, model_ref):
    for h in range(GROUPS):
        image = lax.dot_general(
            every_ref[h * 8 : (h + 1) * 8].reshape(GK, PADPIX),
            select_ref[h],
            (((0,), (0,)), ((), ())),
            preferred_element_type=F32,
        )
        for q in range(QUAD):
            model_ref[q, :, h * GSLOTS : (h + 1) * GSLOTS] = image[
                :, q * GSLOTS : (q + 1) * GSLOTS
            ].astype(BF16)


def accumulate(chunk, xt_ref, own_ref, model_ref, scale_ref, term_ref, rows=16):
    for lane in range(SLOTS // LANES):
        at = slice(lane * LANES, (lane + 1) * LANES)
        quarter = jnp.broadcast_to(scale_ref[0:1, at], (rows, LANES))
        live = jnp.broadcast_to(scale_ref[1:2, at], (rows, LANES))

        def step(i, sums):
            here = pl.ds(pl.multiple_of(i * rows, rows), rows)
            there = pl.ds(pl.multiple_of(chunk * LANES + i * rows, rows), rows)
            x = xt_ref[there, at].astype(F32)
            gap = x - own_ref[here, at]
            weight = live / (1.0 + quarter * (gap * gap))
            m = [model_ref[q, there, at].astype(F32) for q in range(QUAD)]
            wm = [weight * v for v in m]
            new = [wm[q] * m[r] for q, r in PAIRS] + [wm[q] * x for q in range(QUAD)]
            return tuple(s + (v[0:8] + v[8:16]) for s, v in zip(sums, new))

        sums = lax.fori_loop(
            0,
            LANES // rows,
            step,
            tuple(jnp.zeros((8, LANES), F32) for _ in range(14)),
            unroll=UNROLL,
        )
        for n, s in enumerate(sums):
            term_ref[n, :, at] += s


def finish_terms(term_ref, move_ref):
    rows = [jnp.sum(term_ref[n], axis=0, keepdims=True) for n in range(14)]
    block = jnp.concatenate(rows + [jnp.zeros((TERMS - 14, SLOTS), F32)], axis=0)
    moved = jnp.dot(
        jnp.concatenate(halves(block), axis=0), move_ref[...], preferred_element_type=F32
    )
    return moved[0:TERMS] + moved[TERMS : 2 * TERMS] + moved[2 * TERMS : 3 * TERMS]


def invert(mat_ref, zero_ref):
    lane = iota((8, LANES), 1)
    sub = iota((8, LANES), 0)
    zero = zero_ref[...]

    def spread(v, j):
        return jnp.broadcast_to(v[j : j + 1, :], (8, LANES))

    def block(i, _):
        top = pl.multiple_of(i * 8, 8)
        panel = mat_ref[pl.ds(top, 8), :]
        cols = [jnp.broadcast_to(panel[:, k : k + 1], (8, LANES)) + zero for k in range(8)]
        for j in range(8):
            factor = cols[j]
            pivot = 1.0 / spread(factor, j)
            row = jnp.where(lane == j, 1.0, spread(panel, j)) * pivot
            panel = jnp.where(sub == j, row, jnp.where(lane == j, 0.0, panel) - factor * row)
            for k in range(j + 1, 8):
                side = spread(cols[k], j) * pivot
                cols[k] = jnp.where(sub == j, side, cols[k] - factor * side)
        spreads = [spread(panel, j) for j in range(8)]
        for n in range(16):
            old = mat_ref[n * 8 : (n + 1) * 8, :]
            new = jnp.where(lane < 8, 0.0, old)
            even = zero
            for j in range(0, 8, 2):
                new = new - jnp.broadcast_to(old[:, j : j + 1], (8, LANES)) * spreads[j]
                even = even + jnp.broadcast_to(old[:, j + 1 : j + 2], (8, LANES)) * spreads[j + 1]
            new = jnp.where(n == i, panel, new - even)
            mat_ref[n * 8 : (n + 1) * 8, :] = pltpu.roll(new, LANES - 8, 1)
        return 0

    lax.fori_loop(0, 16, block, 0)


def full(a, b):
    return jnp.dot(a, b, preferred_element_type=F32, precision=HIGHEST)


def fill_home(source, home_ref):
    where = iota((ORDER, SLOTS), 0)
    for q in range(QUAD):
        home_ref[q] = (where == source[q : q + 1, :]).astype(F32).astype(BF16)


def halves(v):
    high = v.astype(BF16)
    rest = v - high.astype(F32)
    mid = rest.astype(BF16)
    return high, mid, (rest - mid.astype(F32)).astype(BF16)


def solve(terms, home_ref, side_ref, work_ref, zero_ref):
    gram = jnp.zeros((ORDER, ORDER), F32)
    row = jnp.zeros((8, ORDER), F32)
    for r in range(QUAD):
        for part in range(2):
            mixed = None
            for q in range(r + 1):
                value = terms[PAIRS.index((q, r)) : PAIRS.index((q, r)) + 1, :]
                value = halves(value * (0.5 if q == r else 1.0))[part]
                step = home_ref[q] * value
                mixed = step if mixed is None else mixed + step
            side_ref[part * ORDER : (part + 1) * ORDER, :] = mixed
        one, two, three = halves(terms[10 + r : 11 + r, :])
        side_ref[2 * ORDER : 2 * ORDER + 16, :] = jnp.concatenate(
            [one.astype(F32), two.astype(F32), three.astype(F32), jnp.zeros((13, SLOTS), F32)], axis=0
        ).astype(BF16)
        got = lax.dot_general(
            side_ref[...], home_ref[r], (((1,), (1,)), ((), ())), preferred_element_type=F32
        )
        gram = gram + (got[:ORDER] + got[ORDER : 2 * ORDER])
        row = row + got[2 * ORDER : 2 * ORDER + 8]
    row = row[0:1] + row[1:2] + row[2:3]
    eye = iota((HALF, HALF), 0) == iota((HALF, HALF), 1)
    one = jnp.where(eye, 1.0, 0.0)

    def turn(v):
        return jnp.transpose(jnp.broadcast_to(v, (HALF, HALF)))

    a11 = gram[:HALF, :HALF]
    a22 = gram[HALF:, HALF:]
    a12 = gram[:HALF, HALF:] + jnp.transpose(gram[HALF:, :HALF])
    a21 = jnp.transpose(a12)
    r1_row, r2_row = row[:, :HALF], row[:, HALF:]
    r1_col, r2_col = turn(r1_row)[:, 0:1], turn(r2_row)[:, 0:1]
    work_ref[...] = a11 + jnp.transpose(a11) + one
    invert(work_ref, zero_ref)
    top = work_ref[...]
    tie = full(a21, top)
    work_ref[...] = a22 + jnp.transpose(a22) + one - full(tie, a12)
    invert(work_ref, zero_ref)
    low = work_ref[...]
    v = r2_col - jnp.sum(tie * r1_row, axis=1, keepdims=True)
    f2_row = jnp.sum(low * v, axis=0, keepdims=True)
    f2_col = jnp.sum(low * turn(v)[0:1, :], axis=1, keepdims=True)
    f1_row = jnp.sum(top * r1_col, axis=0, keepdims=True) - jnp.sum(tie * f2_col, axis=0, keepdims=True)
    d2 = jnp.sum(jnp.where(eye, low, 0.0), axis=0, keepdims=True)
    d1 = jnp.sum(jnp.where(eye, top, 0.0), axis=0, keepdims=True) + jnp.sum(
        full(low, tie) * tie, axis=0, keepdims=True
    )
    return f1_row / jnp.sqrt(d1), f2_row / jnp.sqrt(d2)


def remote(src, dst, send, recv, **where):
    return pltpu.make_async_remote_copy(
        src_ref=src, dst_ref=dst, send_sem=send, recv_sem=recv, device_id=where, device_id_type=MESH
    )


def whole_kernel(
    st_ref, cf_ref, iv_ref, cd_ref, src_ref, counts_ref, bases_ref, out_ref,
    mine_ref, key_ref, move_ref, meta_out, meta_in, src_out, src_in, home_ref, side_ref, zero_ref,
    packed, got, every, xt_ref, hot_ref, select_ref, model_ref, scale_ref, own_ref, term_ref,
    tables, parts, mean_own, means, count_ref, terms_out, terms_in, work_ref,
    a_send, a_recv, b_send, b_recv, t_send, t_recv, m_send, m_recv, e_send, e_recv, s_send, s_recv,
):
    me = lax.axis_index("tile")
    g = lax.axis_index("rep")
    x, z, c = me // 16, (me // 2) % 8, me % 2

    def peer(dx, dz, core):
        return (((x + dx + 4) % 4) * 8 + (z + dz + 8) % 8) * 2 + core

    barrier = pltpu.get_barrier_semaphore()

    def greet(o, _):
        pl.semaphore_signal(barrier, inc=1, device_id={"tile": (me + o) % TILES}, device_id_type=MESH)
        return 0

    lax.fori_loop(1, TILES, greet, 0)
    for d in range(1, REPS):
        pl.semaphore_signal(barrier, inc=1, device_id={"rep": (g + d) % REPS}, device_id_type=MESH)

    def send_all(src, dst, n):
        def one(o, _):
            p = (me + o) % TILES
            remote(src.at[p], dst.at[me], a_send.at[n], a_recv.at[n], tile=p).start()
            return 0

        lax.fori_loop(1, TILES, one, 0)
        dst[pl.ds(me, 1)] = src[pl.ds(me, 1)]

    def all_done(src, dst, n):
        many = pl.ds(0, TILES - 1)
        return remote(src.at[many], dst.at[many], a_send.at[n], a_recv.at[n], tile=peer(0, 1, c))

    def send_block(n):
        send_all(packed.at[n], got.at[n], n)

    def block_done(n):
        return all_done(packed.at[n], got.at[n], n)

    def blocks_done(stage, count):
        many = every.at[pl.ds(0, count), 0]
        return remote(many, many, b_send.at[stage], b_recv.at[stage], tile=peer(0, 1, c))

    def send_bases(stage, ref, dx, dz, core):
        remote(ref, ref, b_send.at[stage], b_recv.at[stage], tile=peer(dx, dz, core)).start()

    here = x * 8 + z

    def stage_z1():
        for dz in (1, -1, 2, -2):
            remote(
                mine_ref, every.at[here, c], b_send.at[0], b_recv.at[0], tile=peer(0, dz, c)
            ).start()

    def stage_z2():
        blocks_done(0, 4).wait_recv()
        low = every.at[x * 8 + (z + 6) % 8, c]
        high = every.at[x * 8 + (z + 2) % 8, c]
        send_bases(1, low, 0, 1, c)
        send_bases(1, high, 0, -1, c)
        send_bases(1, low, 0, 2, c)

    def stage_x1():
        blocks_done(1, 3).wait_recv()
        mid = every.at[pl.ds(x * 8, 8), c]
        send_bases(2, mid, 1, 0, c)
        send_bases(2, mid, -1, 0, c)

    def stage_x2():
        blocks_done(2, 16).wait_recv()
        send_bases(3, every.at[pl.ds(((x + 3) % 4) * 8, 4), c], 1, 0, c)
        send_bases(3, every.at[pl.ds(((x + 1) % 4) * 8 + 4, 4), c], -1, 0, c)

    def column(shift):
        return pl.ds(((x + shift) % 4) * 8, 8)

    def stage_core1():
        send_bases(4, every.at[column(0), c], 0, 0, 1 - c)

    def stage_core2():
        send_bases(5, every.at[column(1), c], 0, 0, 1 - c)
        send_bases(5, every.at[column(3), c], 0, 0, 1 - c)

    def stage_core3():
        blocks_done(3, 8).wait_recv()
        send_bases(6, every.at[column(2), c], 0, 0, 1 - c)

    def stack(n):
        block_done(n).wait_recv()
        turned = jnp.transpose(got[n].reshape(SLOTS, LANES).astype(F32)).astype(BF16)
        xt_ref[n * LANES : (n + 1) * LANES, :] = turned
        part = lax.dot_general(
            turned, hot_ref[...], (((1,), (1,)), ((), ())), preferred_element_type=F32
        )
        for b in range(REPS):
            tables[n, b] = part[:, b * ORDER : (b + 1) * ORDER].astype(BF16)
        for d in range(1, REPS):
            b = (g + d) % REPS
            remote(tables.at[n, b], parts.at[n, g], t_send.at[n], t_recv.at[n], rep=b).start()
        parts[n, pl.ds(g, 1)] = tables[n, pl.ds(g, 1)]

    def three(src, dst, send, recv, n):
        many = pl.ds(0, REPS - 1)
        return remote(src.at[n, many], dst.at[n, many], send.at[n], recv.at[n], rep=(g + 1) % REPS)

    def mean(n):
        three(tables, parts, t_send, t_recv, n).wait_recv()
        total = parts[n, 0].astype(F32)
        for other in range(1, REPS):
            total = total + parts[n, other].astype(F32)
        if n == CHUNKS - 1:
            at = PIX - (CHUNKS - 1) * LANES
            count_ref[...] = jnp.broadcast_to(total[at : at + 1, :], (8, ORDER))
        value = (total / (1.0 + count_ref[0:1, :])).astype(BF16)
        mean_own[n, 0] = value
        for d in range(1, REPS):
            remote(
                mean_own.at[n, 0], means.at[n, g], m_send.at[n], m_recv.at[n], rep=(g + d) % REPS
            ).start()
        means[n, pl.ds(g, 1)] = mean_own[n]

    def terms(n):
        three(means, means, m_send, m_recv, n).wait_recv()
        joined = jnp.concatenate([means[n, b] for b in range(REPS)], axis=1)
        own_ref[...] = jnp.dot(joined, hot_ref[...], preferred_element_type=F32)
        accumulate(n, xt_ref, own_ref, model_ref, scale_ref, term_ref)

    pack_meta(cf_ref, iv_ref, cd_ref, meta_out)
    pack_block(st_ref, 4, packed)
    mine_ref[...] = jnp.zeros_like(mine_ref)
    mine_ref[0 : CCD * BASIS, 0:PIX] = jnp.concatenate(
        [bases_ref[k].astype(F32) for k in range(BASIS)], axis=0
    ).astype(BF16)
    pl.semaphore_wait(barrier, TILES - 1 + REPS - 1)
    stage_z1()
    send_all(meta_out, meta_in, CHUNKS)
    send_block(4)
    every[pl.ds(here, 1), pl.ds(c, 1)] = mine_ref[...].reshape(1, 1, ROWS, PADPIX)
    pack_block(st_ref, 0, packed)
    stage_z2()
    send_block(0)
    pack_block(st_ref, 1, packed)
    stage_x1()
    stage_core1()
    send_block(1)
    pack_block(st_ref, 2, packed)
    pack_block(st_ref, 3, packed)
    send_block(2)
    fill_key(counts_ref, src_ref, key_ref)
    fill_hot(key_ref, hot_ref)
    fill_move(move_ref)
    wide = jnp.concatenate([src_ref[...].astype(F32), jnp.zeros((12, SLOTS), F32)], axis=0)
    wide = jnp.dot(wide.astype(BF16), move_ref[...], preferred_element_type=F32)
    for b in range(REPS):
        src_out[0, b] = wide[0:8, b * ORDER : (b + 1) * ORDER]
    for d in range(1, REPS):
        b = (g + d) % REPS
        remote(src_out.at[0, b], src_in.at[0, g], s_send.at[0], s_recv.at[0], rep=b).start()
    src_in[0, pl.ds(g, 1)] = src_out[0, pl.ds(g, 1)]
    stage_x2()
    stage_core2()
    send_block(3)
    term_ref[...] = jnp.zeros_like(term_ref)
    zero_ref[...] = jnp.zeros_like(zero_ref)
    all_done(meta_out, meta_in, CHUNKS).wait_recv()
    meta = unpack_meta(meta_in)
    ivar = meta[QUAD * BASIS : QUAD * BASIS + 1, :]
    scale_ref[0:1, :] = ivar * 0.25
    scale_ref[1:2, :] = jnp.where(key_ref[...] >= 0, ivar, 0.0)
    fill_select(meta, select_ref)
    stack(4)
    stage_core3()
    stack(0)
    mean(4)
    three(src_out, src_in, s_send, s_recv, 0).wait_recv()
    fill_home(
        jnp.concatenate([src_in[0, k] for k in range(REPS)], axis=1).astype(I32), home_ref
    )
    stack(1)
    mean(0)
    stack(2)
    mean(1)
    blocks_done(4, 8).wait_recv()
    blocks_done(5, 16).wait_recv()
    blocks_done(6, 8).wait_recv()
    render(every, select_ref, model_ref)
    terms(4)
    stack(3)
    mean(2)
    terms(0)
    terms(1)
    mean(3)
    terms(2)
    terms(3)
    block = finish_terms(term_ref, move_ref)
    for b in range(REPS):
        terms_out[0, b] = block[:, b * ORDER : (b + 1) * ORDER]
    for d in range(1, REPS):
        b = (g + d) % REPS
        remote(terms_out.at[0, b], terms_in.at[0, g], e_send.at[0], e_recv.at[0], rep=b).start()
    terms_in[0, pl.ds(g, 1)] = terms_out[0, pl.ds(g, 1)]
    three(terms_out, terms_in, e_send, e_recv, 0).wait_recv()
    joined = jnp.concatenate([terms_in[0, k] for k in range(REPS)], axis=1)
    left, right = solve(joined, home_ref, side_ref, work_ref, zero_ref)
    out_ref[:, :HALF] = left
    out_ref[:, HALF:] = right

    for n in range(CHUNKS):
        block_done(n).wait_send()
    all_done(meta_out, meta_in, CHUNKS).wait_send()
    three(src_out, src_in, s_send, s_recv, 0).wait_send()
    for stage, count in enumerate((4, 3, 16, 8, 8, 16, 8)):
        blocks_done(stage, count).wait_send()
    for n in range(CHUNKS):
        three(tables, parts, t_send, t_recv, n).wait_send()
        three(means, means, m_send, m_recv, n).wait_send()
    three(terms_out, terms_in, e_send, e_recv, 0).wait_send()


def struct(shape, dtype):
    return jax.ShapeDtypeStruct(shape, dtype)


def local(stamps, coefs, ivar, ccd, bases, sources, counts):
    dma = pltpu.SemaphoreType.DMA
    return pl.pallas_call(
        whole_kernel,
        out_shape=struct((1, ORDER), F32),
        in_specs=[VMEM] * 7,
        out_specs=VMEM,
        scratch_shapes=[
            pltpu.VMEM((ROWS, PADPIX), BF16),
            pltpu.VMEM((1, SLOTS), I32),
            pltpu.VMEM((SLOTS, SLOTS), BF16),
            pltpu.VMEM((TILES, 8, LANES), BF16),
            pltpu.VMEM((TILES, 8, LANES), BF16),
            pltpu.VMEM((1, REPS, 8, ORDER), F32),
            pltpu.VMEM((1, REPS, 8, ORDER), F32),
            pltpu.VMEM((QUAD, ORDER, SLOTS), BF16),
            pltpu.VMEM((2 * ORDER + 16, SLOTS), BF16),
            pltpu.VMEM((8, LANES), F32),
            pltpu.VMEM((CHUNKS, TILES, 16, LANES), BF16),
            pltpu.VMEM((CHUNKS, TILES, 16, LANES), BF16),
            pltpu.VMEM((32, 2, ROWS, PADPIX), BF16),
            pltpu.VMEM((PADPIX, SLOTS), BF16),
            pltpu.VMEM((SLOTS, SLOTS), BF16),
            pltpu.VMEM((GROUPS, GK, QUAD * GSLOTS), BF16),
            pltpu.VMEM((QUAD, PADPIX, SLOTS), BF16),
            pltpu.VMEM((8, SLOTS), F32),
            pltpu.VMEM((LANES, SLOTS), F32),
            pltpu.VMEM((14, 8, SLOTS), F32),
            pltpu.VMEM((CHUNKS, REPS, LANES, ORDER), BF16),
            pltpu.VMEM((CHUNKS, REPS, LANES, ORDER), BF16),
            pltpu.VMEM((CHUNKS, 1, LANES, ORDER), BF16),
            pltpu.VMEM((CHUNKS, REPS, LANES, ORDER), BF16),
            pltpu.VMEM((8, ORDER), F32),
            pltpu.VMEM((1, REPS, TERMS, ORDER), F32),
            pltpu.VMEM((1, REPS, TERMS, ORDER), F32),
            pltpu.VMEM((HALF, HALF), F32),
            dma((CHUNKS + 1,)),
            dma((CHUNKS + 1,)),
            dma((7,)),
            dma((7,)),
            dma((CHUNKS,)),
            dma((CHUNKS,)),
            dma((CHUNKS,)),
            dma((CHUNKS,)),
            dma((1,)),
            dma((1,)),
            dma((1,)),
            dma((1,)),
        ],
        compiler_params=pltpu.CompilerParams(
            collective_id=0, has_side_effects=True, vmem_limit_bytes=60 * 1024 * 1024
        ),
    )(
        stamps,
        jnp.transpose(coefs, (1, 0, 2)),
        ivar.reshape(8, LANES),
        ccd.reshape(8, LANES),
        sources,
        jnp.transpose(counts),
        jnp.transpose(bases, (1, 0, 2)),
    )


def solution(mesh):
    return jax.shard_map(
        local,
        mesh=mesh,
        in_specs=(
            P(None, ("tile", "rep")),
            P(None, None, ("tile", "rep")),
            P(("tile", "rep")),
            P(("tile", "rep")),
            P(("tile", "rep"), None, None),
            P(None, ("tile", "rep")),
            P(("tile", "rep"), None),
        ),
        out_specs=P(("tile", "rep"), None),
        check_vma=False,
    )
```

```python
import functools

import jax
import jax.numpy as jnp
from jax import lax
from jax.experimental import pallas as pl
from jax.experimental.pallas import tpu as pltpu
from jax.sharding import PartitionSpec as P

F32 = jnp.float32
BF16 = jnp.bfloat16
I32 = jnp.int32
HIGHEST = lax.Precision.HIGHEST

PIX = 625
LANES = 128
CHUNKS = 5
PADPIX = CHUNKS * LANES
TILES = 64
REPS = 4
SLOTS = 1024
BASIS = 10
QUAD = 4
CCD = 4
GROUP = 16
GROUPS = TILES // GROUP
GSLOTS = GROUP * 16
ROWS = 48
GK = GROUP * ROWS
ORDER = 256
HALF = 128
TERMS = 16
UNROLL = 2
PAIRS = [(q, r) for q in range(QUAD) for r in range(q, QUAD)]
MESH = pl.DeviceIdType.MESH
VMEM = pl.BlockSpec(memory_space=pltpu.VMEM)


def iota(shape, axis):
    return lax.broadcasted_iota(I32, shape, axis)


def flat(ref):
    return jnp.concatenate([ref[i : i + 1, :].astype(F32) for i in range(8)], axis=1)


def pack_meta(cf_ref, iv_ref, cd_ref, out_ref):
    meta = jnp.concatenate(
        [cf_ref[k].astype(F32) for k in range(BASIS)]
        + [flat(iv_ref), flat(cd_ref), jnp.zeros((LANES - QUAD * BASIS - 2, SLOTS), F32)],
        axis=0,
    )
    rows = jnp.transpose(meta).reshape(TILES, 16, LANES)
    left = rows[:, :8].reshape(TILES * 8, LANES)
    right = rows[:, 8:].reshape(TILES * 8, LANES)
    out_ref[...] = (left + pltpu.roll(right, 64, 1)).reshape(TILES, 8, LANES).astype(BF16)


def unpack_meta(got_ref):
    rows = got_ref[...].astype(F32)
    other = pltpu.roll(rows.reshape(TILES * 8, LANES), 64, 1).reshape(TILES, 8, LANES)
    return jnp.transpose(jnp.concatenate([rows, other], axis=1).reshape(SLOTS, LANES))


def pack_block(st_ref, chunk, out_ref):
    if chunk < CHUNKS - 1:
        block = st_ref[chunk * LANES : (chunk + 1) * LANES, :].astype(F32)
    else:
        body = st_ref[chunk * LANES : PIX - 1, :].astype(F32)
        last = jnp.broadcast_to(st_ref[PIX - 1 : PIX, :].astype(F32), (16, SLOTS))
        row = iota((16, SLOTS), 0)
        tail = jnp.where(row == 0, last, jnp.where(row == 1, 1.0, 0.0))
        block = jnp.concatenate([body, tail], axis=0)
    out_ref[chunk] = jnp.transpose(block).astype(BF16).reshape(TILES, 16, LANES)


def fill_key(counts_ref, src_ref, key_ref):
    owner = (iota((TILES, SLOTS), 0) == iota((TILES, SLOTS), 1) // 16).astype(F32).astype(BF16)
    count = jnp.concatenate(
        [counts_ref[...].astype(F32), jnp.zeros((12, TILES), F32)], axis=0
    ).astype(BF16)
    laid = jnp.dot(count, owner, preferred_element_type=F32)
    lane = iota((1, SLOTS), 1)
    blob = (lane // 4) % 4
    mine = jnp.zeros((1, SLOTS), F32)
    for b in range(REPS):
        mine = jnp.where(blob == b, laid[b : b + 1, :], mine)
    live = (lane % 4).astype(F32) < mine
    key_ref[...] = jnp.where(live, src_ref[0:1, :] + blob * ORDER, -1)


def fill_move(move_ref):
    row = iota((SLOTS, 1), 0)
    home = ((row // 4) % 4) * ORDER + (row // 16) * 4 + row % 4
    move_ref[...] = (home == iota((SLOTS, SLOTS), 1)).astype(F32).astype(BF16)


def fill_hot(key_ref, hot_ref):
    hot_ref[...] = (iota((SLOTS, SLOTS), 0) == key_ref[...]).astype(F32).astype(BF16)


def fill_select(meta, select_ref):
    cols = meta.astype(BF16)
    image = iota((ROWS, 1), 0)
    own_ccd = jnp.where(image < CCD * BASIS, image % CCD, -1).astype(F32)
    hit = own_ccd == meta[QUAD * BASIS + 1 : QUAD * BASIS + 2, :]
    owner = iota((16, GSLOTS), 1) // 16
    laid = []
    for q in range(QUAD):
        spread = (iota((ROWS, LANES), 1) == (image // CCD) * QUAD + q).astype(F32).astype(BF16)
        value = jnp.dot(spread, cols, preferred_element_type=F32)
        laid.append(jnp.where(hit, value, 0.0).astype(BF16))
    for t in range(GROUP):
        seen = (owner == t).astype(F32).astype(BF16)
        for h in range(GROUPS):
            for q in range(QUAD):
                for part in range(ROWS // 16):
                    select_ref[
                        h,
                        t * ROWS + part * 16 : t * ROWS + (part + 1) * 16,
                        q * GSLOTS : (q + 1) * GSLOTS,
                    ] = seen * laid[q][part * 16 : (part + 1) * 16, h * GSLOTS : (h + 1) * GSLOTS]


def render(h, every_ref, select_ref, model_ref):
    image = lax.dot_general(
        every_ref[pl.ds(h * 8, 8)].reshape(GK, PADPIX),
        select_ref[h],
        (((0,), (0,)), ((), ())),
        preferred_element_type=F32,
    )
    at = pl.ds(pl.multiple_of(h * GSLOTS, GSLOTS), GSLOTS)
    for q in range(QUAD):
        model_ref[q, :, at] = image[:, q * GSLOTS : (q + 1) * GSLOTS].astype(BF16)


def accumulate(chunk, xt_ref, own_ref, model_ref, scale_ref, term_ref, rows=16):
    for lane in range(SLOTS // LANES):
        at = slice(lane * LANES, (lane + 1) * LANES)
        quarter = jnp.broadcast_to(scale_ref[0:1, at], (rows, LANES))
        live = jnp.broadcast_to(scale_ref[1:2, at], (rows, LANES))

        def step(i, sums):
            here = pl.ds(pl.multiple_of(i * rows, rows), rows)
            there = pl.ds(pl.multiple_of(chunk * LANES + i * rows, rows), rows)
            x = xt_ref[there, at].astype(F32)
            gap = x - own_ref[here, at]
            weight = live / (1.0 + quarter * (gap * gap))
            m = [model_ref[q, there, at].astype(F32) for q in range(QUAD)]
            wm = [weight * v for v in m]
            new = [wm[q] * m[r] for q, r in PAIRS] + [wm[q] * x for q in range(QUAD)]
            return tuple(s + (v[0:8] + v[8:16]) for s, v in zip(sums, new))

        sums = lax.fori_loop(
            0,
            LANES // rows,
            step,
            tuple(jnp.zeros((8, LANES), F32) for _ in range(14)),
            unroll=UNROLL,
        )
        for n, s in enumerate(sums):
            term_ref[n, :, at] += s


def finish_terms(term_ref, move_ref):
    rows = [jnp.sum(term_ref[n], axis=0, keepdims=True) for n in range(14)]
    block = jnp.concatenate(rows + [jnp.zeros((TERMS - 14, SLOTS), F32)], axis=0)
    moved = jnp.dot(
        jnp.concatenate(halves(block), axis=0), move_ref[...], preferred_element_type=F32
    )
    return moved[0:TERMS] + moved[TERMS : 2 * TERMS] + moved[2 * TERMS : 3 * TERMS]


def invert(mat_ref, zero_ref):
    lane = iota((8, LANES), 1)
    sub = iota((8, LANES), 0)
    zero = zero_ref[...]

    def spread(v, j):
        return jnp.broadcast_to(v[j : j + 1, :], (8, LANES))

    def block(o, _):
        top = pl.multiple_of(o * 32, 32)
        rows = [mat_ref[pl.ds(top + 8 * m, 8), :] for m in range(4)]
        for kb in range(4):
            base = 8 * kb
            panel = rows[kb]
            cols = [
                jnp.broadcast_to(panel[:, base + k : base + k + 1], (8, LANES)) + zero
                for k in range(8)
            ]
            for j in range(8):
                factor = cols[j]
                pivot = 1.0 / spread(factor, j)
                row = jnp.where(lane == base + j, 1.0, spread(panel, j)) * pivot
                kept = jnp.where(lane == base + j, 0.0, panel)
                panel = jnp.where(sub == j, row, kept - factor * row)
                for k in range(j + 1, 8):
                    side = spread(cols[k], j) * pivot
                    cols[k] = jnp.where(sub == j, side, cols[k] - factor * side)
            spreads = [spread(panel, j) for j in range(8)]
            rows[kb] = panel
            for m in range(4):
                if m == kb:
                    continue
                old = rows[m]
                new = jnp.where((lane >= base) & (lane < base + 8), 0.0, old)
                even = zero
                for j in range(0, 8, 2):
                    a = jnp.broadcast_to(old[:, base + j : base + j + 1], (8, LANES))
                    b = jnp.broadcast_to(old[:, base + j + 1 : base + j + 2], (8, LANES))
                    new = new - a * spreads[j]
                    even = even + b * spreads[j + 1]
                rows[m] = new - even
        whole = mat_ref[...]
        done = jnp.concatenate(rows, axis=0)
        kept = jnp.where(iota((HALF, LANES), 1) < 32, 0.0, whole)
        mat_ref[...] = pltpu.roll(kept - full(whole[:, 0:32], done), LANES - 32, 1)
        mat_ref[pl.ds(top, 32), :] = pltpu.roll(done, LANES - 32, 1)
        return 0

    lax.fori_loop(0, 4, block, 0)


def full(a, b):
    return jnp.dot(a, b, preferred_element_type=F32, precision=HIGHEST)


def fill_home(source, home_ref):
    where = iota((ORDER, SLOTS), 0)
    for q in range(QUAD):
        home_ref[q] = (where == source[q : q + 1, :]).astype(F32).astype(BF16)


def halves(v):
    high = v.astype(BF16)
    rest = v - high.astype(F32)
    mid = rest.astype(BF16)
    return high, mid, (rest - mid.astype(F32)).astype(BF16)


def solve(terms, home_ref, side_ref, work_ref, zero_ref):
    gram = jnp.zeros((ORDER, ORDER), F32)
    row = jnp.zeros((8, ORDER), F32)
    for r in range(QUAD):
        for part in range(2):
            mixed = None
            for q in range(r + 1):
                value = terms[PAIRS.index((q, r)) : PAIRS.index((q, r)) + 1, :]
                value = halves(value * (0.5 if q == r else 1.0))[part]
                step = home_ref[q] * value
                mixed = step if mixed is None else mixed + step
            side_ref[part * ORDER : (part + 1) * ORDER, :] = mixed
        one, two, three = halves(terms[10 + r : 11 + r, :])
        side_ref[2 * ORDER : 2 * ORDER + 16, :] = jnp.concatenate(
            [one.astype(F32), two.astype(F32), three.astype(F32), jnp.zeros((13, SLOTS), F32)], axis=0
        ).astype(BF16)
        got = lax.dot_general(
            side_ref[...], home_ref[r], (((1,), (1,)), ((), ())), preferred_element_type=F32
        )
        gram = gram + (got[:ORDER] + got[ORDER : 2 * ORDER])
        row = row + got[2 * ORDER : 2 * ORDER + 8]
    row = row[0:1] + row[1:2] + row[2:3]
    eye = iota((HALF, HALF), 0) == iota((HALF, HALF), 1)
    one = jnp.where(eye, 1.0, 0.0)

    def turn(v):
        return jnp.transpose(jnp.broadcast_to(v, (HALF, HALF)))

    a11 = gram[:HALF, :HALF]
    a22 = gram[HALF:, HALF:]
    a12 = gram[:HALF, HALF:] + jnp.transpose(gram[HALF:, :HALF])
    a21 = jnp.transpose(a12)
    r1_row, r2_row = row[:, :HALF], row[:, HALF:]
    r1_col, r2_col = turn(r1_row)[:, 0:1], turn(r2_row)[:, 0:1]
    work_ref[...] = a11 + jnp.transpose(a11) + one
    invert(work_ref, zero_ref)
    top = work_ref[...]
    tie = full(a21, top)
    work_ref[...] = a22 + jnp.transpose(a22) + one - full(tie, a12)
    invert(work_ref, zero_ref)
    low = work_ref[...]
    v = r2_col - jnp.sum(tie * r1_row, axis=1, keepdims=True)
    f2_row = jnp.sum(low * v, axis=0, keepdims=True)
    f2_col = jnp.sum(low * turn(v)[0:1, :], axis=1, keepdims=True)
    f1_row = jnp.sum(top * r1_col, axis=0, keepdims=True) - jnp.sum(tie * f2_col, axis=0, keepdims=True)
    d2 = jnp.sum(jnp.where(eye, low, 0.0), axis=0, keepdims=True)
    d1 = jnp.sum(jnp.where(eye, top, 0.0), axis=0, keepdims=True) + jnp.sum(
        full(low, tie) * tie, axis=0, keepdims=True
    )
    return f1_row / jnp.sqrt(d1), f2_row / jnp.sqrt(d2)


def remote(src, dst, send, recv, **where):
    return pltpu.make_async_remote_copy(
        src_ref=src, dst_ref=dst, send_sem=send, recv_sem=recv, device_id=where, device_id_type=MESH
    )


def whole_kernel(
    st_ref, cf_ref, iv_ref, cd_ref, src_ref, counts_ref, bases_ref, out_ref,
    mine_ref, key_ref, move_ref, meta_out, meta_in, src_out, src_in, home_ref, side_ref, zero_ref,
    packed, got, every, xt_ref, hot_ref, select_ref, model_ref, scale_ref, own_ref, term_ref,
    tables, parts, mean_own, means, count_ref, terms_out, terms_in, work_ref,
    a_send, a_recv, b_send, b_recv, t_send, t_recv, m_send, m_recv, e_send, e_recv, s_send, s_recv,
):
    me = lax.axis_index("tile")
    g = lax.axis_index("rep")
    x, z, c = me // 16, (me // 2) % 8, me % 2

    def peer(dx, dz, core):
        return (((x + dx + 4) % 4) * 8 + (z + dz + 8) % 8) * 2 + core

    barrier = pltpu.get_barrier_semaphore()

    def greet(o, _):
        pl.semaphore_signal(barrier, inc=1, device_id={"tile": (me + o) % TILES}, device_id_type=MESH)
        return 0

    lax.fori_loop(1, TILES, greet, 0)
    for d in range(1, REPS):
        pl.semaphore_signal(barrier, inc=1, device_id={"rep": (g + d) % REPS}, device_id_type=MESH)

    def send_all(src, dst, n):
        def one(o, _):
            p = (me + o) % TILES
            remote(src.at[p], dst.at[me], a_send.at[n], a_recv.at[n], tile=p).start()
            return 0

        lax.fori_loop(1, TILES, one, 0)
        dst[pl.ds(me, 1)] = src[pl.ds(me, 1)]

    def all_done(src, dst, n):
        many = pl.ds(0, TILES - 1)
        return remote(src.at[many], dst.at[many], a_send.at[n], a_recv.at[n], tile=peer(0, 1, c))

    def send_block(n):
        send_all(packed.at[n], got.at[n], n)

    def block_done(n):
        return all_done(packed.at[n], got.at[n], n)

    def blocks_done(stage, count):
        many = every.at[pl.ds(0, count), 0]
        return remote(many, many, b_send.at[stage], b_recv.at[stage], tile=peer(0, 1, c))

    def send_bases(stage, ref, dx, dz, core):
        remote(ref, ref, b_send.at[stage], b_recv.at[stage], tile=peer(dx, dz, core)).start()

    here = x * 8 + z

    def origin(dx, dz):
        return every.at[((x + dx + 4) % 4) * 8 + (z + dz + 8) % 8, c]

    def stage_z1():
        for dz in (1, -1, 2, -2):
            remote(
                mine_ref, every.at[here, c], b_send.at[0], b_recv.at[0], tile=peer(0, dz, c)
            ).start()

    def stage_z2():
        send_bases(1, origin(0, -2), 0, 1, c)
        send_bases(1, origin(0, 2), 0, -1, c)
        send_bases(1, origin(0, -2), 0, 2, c)

    def stage_x1(stage, offsets):
        for dz in offsets:
            for dx in (1, -1):
                send_bases(stage, origin(0, dz), dx, 0, c)

    def stage_x2(stage, ahead, back):
        for dz in ahead:
            send_bases(stage, origin(-1, dz), 1, 0, c)
        for dz in back:
            send_bases(stage, origin(1, dz), -1, 0, c)

    def column(shift):
        return pl.ds(((x + shift) % 4) * 8, 8)

    def stage_core1():
        send_bases(4, every.at[column(0), c], 0, 0, 1 - c)

    def stage_core2():
        send_bases(5, every.at[column(1), c], 0, 0, 1 - c)
        send_bases(5, every.at[column(3), c], 0, 0, 1 - c)

    def stage_core3():
        blocks_done(3, 5).wait_recv()
        blocks_done(8, 3).wait_recv()
        send_bases(6, every.at[column(2), c], 0, 0, 1 - c)

    def show(shift):
        render((x + shift) % 4, every, select_ref, model_ref)

    def stack(n):
        block_done(n).wait_recv()
        turned = jnp.transpose(got[n].reshape(SLOTS, LANES).astype(F32)).astype(BF16)
        xt_ref[n * LANES : (n + 1) * LANES, :] = turned
        part = lax.dot_general(
            turned, hot_ref[...], (((1,), (1,)), ((), ())), preferred_element_type=F32
        )
        for b in range(REPS):
            tables[n, b] = part[:, b * ORDER : (b + 1) * ORDER].astype(BF16)
        for d in range(1, REPS):
            b = (g + d) % REPS
            remote(tables.at[n, b], parts.at[n, g], t_send.at[n], t_recv.at[n], rep=b).start()
        parts[n, pl.ds(g, 1)] = tables[n, pl.ds(g, 1)]

    def three(src, dst, send, recv, n):
        many = pl.ds(0, REPS - 1)
        return remote(src.at[n, many], dst.at[n, many], send.at[n], recv.at[n], rep=(g + 1) % REPS)

    def mean(n):
        three(tables, parts, t_send, t_recv, n).wait_recv()
        total = parts[n, 0].astype(F32)
        for other in range(1, REPS):
            total = total + parts[n, other].astype(F32)
        if n == CHUNKS - 1:
            at = PIX - (CHUNKS - 1) * LANES
            count_ref[...] = jnp.broadcast_to(total[at : at + 1, :], (8, ORDER))
        value = (total / (1.0 + count_ref[0:1, :])).astype(BF16)
        mean_own[n, 0] = value
        for d in range(1, REPS):
            remote(
                mean_own.at[n, 0], means.at[n, g], m_send.at[n], m_recv.at[n], rep=(g + d) % REPS
            ).start()
        means[n, pl.ds(g, 1)] = mean_own[n]

    def terms(n):
        three(means, means, m_send, m_recv, n).wait_recv()
        joined = jnp.concatenate([means[n, b] for b in range(REPS)], axis=1)
        own_ref[...] = jnp.dot(joined, hot_ref[...], preferred_element_type=F32)
        accumulate(n, xt_ref, own_ref, model_ref, scale_ref, term_ref)

    pack_meta(cf_ref, iv_ref, cd_ref, meta_out)
    pack_block(st_ref, 4, packed)
    mine_ref[...] = jnp.zeros_like(mine_ref)
    mine_ref[0 : CCD * BASIS, 0:PIX] = jnp.concatenate(
        [bases_ref[k].astype(F32) for k in range(BASIS)], axis=0
    ).astype(BF16)
    pl.semaphore_wait(barrier, TILES - 1 + REPS - 1)
    stage_z1()
    every[pl.ds(here, 1), pl.ds(c, 1)] = mine_ref[...].reshape(1, 1, ROWS, PADPIX)
    pack_block(st_ref, 0, packed)
    blocks_done(0, 4).wait_recv()
    stage_z2()
    stage_x1(2, (0, 1, -1, 2, -2))
    send_all(meta_out, meta_in, CHUNKS)
    send_block(4)
    pack_block(st_ref, 1, packed)
    blocks_done(1, 3).wait_recv()
    stage_x1(7, (3, 4, -3))
    stage_core1()
    send_block(0)
    send_block(1)
    pack_block(st_ref, 2, packed)
    pack_block(st_ref, 3, packed)
    blocks_done(2, 10).wait_recv()
    stage_x2(3, (0, 1, 2), (-1, -2))
    blocks_done(7, 6).wait_recv()
    stage_x2(8, (3, 4), (-3,))
    stage_core2()
    send_block(2)
    send_block(3)
    fill_key(counts_ref, src_ref, key_ref)
    fill_hot(key_ref, hot_ref)
    fill_move(move_ref)
    wide = jnp.concatenate([src_ref[...].astype(F32), jnp.zeros((12, SLOTS), F32)], axis=0)
    wide = jnp.dot(wide.astype(BF16), move_ref[...], preferred_element_type=F32)
    for b in range(REPS):
        src_out[0, b] = wide[0:8, b * ORDER : (b + 1) * ORDER]
    for d in range(1, REPS):
        b = (g + d) % REPS
        remote(src_out.at[0, b], src_in.at[0, g], s_send.at[0], s_recv.at[0], rep=b).start()
    src_in[0, pl.ds(g, 1)] = src_out[0, pl.ds(g, 1)]
    term_ref[...] = jnp.zeros_like(term_ref)
    zero_ref[...] = jnp.zeros_like(zero_ref)
    all_done(meta_out, meta_in, CHUNKS).wait_recv()
    meta = unpack_meta(meta_in)
    ivar = meta[QUAD * BASIS : QUAD * BASIS + 1, :]
    scale_ref[0:1, :] = ivar * 0.25
    scale_ref[1:2, :] = jnp.where(key_ref[...] >= 0, ivar, 0.0)
    fill_select(meta, select_ref)
    blocks_done(4, 8).wait_recv()
    show(0)
    stack(4)
    three(src_out, src_in, s_send, s_recv, 0).wait_recv()
    fill_home(
        jnp.concatenate([src_in[0, k] for k in range(REPS)], axis=1).astype(I32), home_ref
    )
    stack(0)
    mean(4)
    blocks_done(5, 16).wait_recv()
    show(1)
    show(3)
    stack(1)
    mean(0)
    stage_core3()
    stack(2)
    mean(1)
    blocks_done(6, 8).wait_recv()
    show(2)
    terms(4)
    stack(3)
    mean(2)
    terms(0)
    terms(1)
    mean(3)
    terms(2)
    terms(3)
    block = finish_terms(term_ref, move_ref)
    for b in range(REPS):
        terms_out[0, b] = block[:, b * ORDER : (b + 1) * ORDER]
    for d in range(1, REPS):
        b = (g + d) % REPS
        remote(terms_out.at[0, b], terms_in.at[0, g], e_send.at[0], e_recv.at[0], rep=b).start()
    terms_in[0, pl.ds(g, 1)] = terms_out[0, pl.ds(g, 1)]
    three(terms_out, terms_in, e_send, e_recv, 0).wait_recv()
    joined = jnp.concatenate([terms_in[0, k] for k in range(REPS)], axis=1)
    left, right = solve(joined, home_ref, side_ref, work_ref, zero_ref)
    out_ref[:, :HALF] = left
    out_ref[:, HALF:] = right

    for n in range(CHUNKS):
        block_done(n).wait_send()
    all_done(meta_out, meta_in, CHUNKS).wait_send()
    three(src_out, src_in, s_send, s_recv, 0).wait_send()
    for stage, count in enumerate((4, 3, 10, 5, 8, 16, 8, 6, 3)):
        blocks_done(stage, count).wait_send()
    for n in range(CHUNKS):
        three(tables, parts, t_send, t_recv, n).wait_send()
        three(means, means, m_send, m_recv, n).wait_send()
    three(terms_out, terms_in, e_send, e_recv, 0).wait_send()


def struct(shape, dtype):
    return jax.ShapeDtypeStruct(shape, dtype)


def local(stamps, coefs, ivar, ccd, bases, sources, counts):
    dma = pltpu.SemaphoreType.DMA
    return pl.pallas_call(
        whole_kernel,
        out_shape=struct((1, ORDER), F32),
        in_specs=[VMEM] * 7,
        out_specs=VMEM,
        scratch_shapes=[
            pltpu.VMEM((ROWS, PADPIX), BF16),
            pltpu.VMEM((1, SLOTS), I32),
            pltpu.VMEM((SLOTS, SLOTS), BF16),
            pltpu.VMEM((TILES, 8, LANES), BF16),
            pltpu.VMEM((TILES, 8, LANES), BF16),
            pltpu.VMEM((1, REPS, 8, ORDER), F32),
            pltpu.VMEM((1, REPS, 8, ORDER), F32),
            pltpu.VMEM((QUAD, ORDER, SLOTS), BF16),
            pltpu.VMEM((2 * ORDER + 16, SLOTS), BF16),
            pltpu.VMEM((8, LANES), F32),
            pltpu.VMEM((CHUNKS, TILES, 16, LANES), BF16),
            pltpu.VMEM((CHUNKS, TILES, 16, LANES), BF16),
            pltpu.VMEM((32, 2, ROWS, PADPIX), BF16),
            pltpu.VMEM((PADPIX, SLOTS), BF16),
            pltpu.VMEM((SLOTS, SLOTS), BF16),
            pltpu.VMEM((GROUPS, GK, QUAD * GSLOTS), BF16),
            pltpu.VMEM((QUAD, PADPIX, SLOTS), BF16),
            pltpu.VMEM((8, SLOTS), F32),
            pltpu.VMEM((LANES, SLOTS), F32),
            pltpu.VMEM((14, 8, SLOTS), F32),
            pltpu.VMEM((CHUNKS, REPS, LANES, ORDER), BF16),
            pltpu.VMEM((CHUNKS, REPS, LANES, ORDER), BF16),
            pltpu.VMEM((CHUNKS, 1, LANES, ORDER), BF16),
            pltpu.VMEM((CHUNKS, REPS, LANES, ORDER), BF16),
            pltpu.VMEM((8, ORDER), F32),
            pltpu.VMEM((1, REPS, TERMS, ORDER), F32),
            pltpu.VMEM((1, REPS, TERMS, ORDER), F32),
            pltpu.VMEM((HALF, HALF), F32),
            dma((CHUNKS + 1,)),
            dma((CHUNKS + 1,)),
            dma((9,)),
            dma((9,)),
            dma((CHUNKS,)),
            dma((CHUNKS,)),
            dma((CHUNKS,)),
            dma((CHUNKS,)),
            dma((1,)),
            dma((1,)),
            dma((1,)),
            dma((1,)),
        ],
        compiler_params=pltpu.CompilerParams(
            collective_id=0, has_side_effects=True, vmem_limit_bytes=60 * 1024 * 1024
        ),
    )(
        stamps,
        jnp.transpose(coefs, (1, 0, 2)),
        ivar.reshape(8, LANES),
        ccd.reshape(8, LANES),
        sources,
        jnp.transpose(counts),
        jnp.transpose(bases, (1, 0, 2)),
    )


def solution(mesh):
    return jax.shard_map(
        local,
        mesh=mesh,
        in_specs=(
            P(None, ("tile", "rep")),
            P(None, None, ("tile", "rep")),
            P(("tile", "rep")),
            P(("tile", "rep")),
            P(("tile", "rep"), None, None),
            P(None, ("tile", "rep")),
            P(("tile", "rep"), None),
        ),
        out_specs=P(("tile", "rep"), None),
        check_vma=False,
    )
```

```python
import functools

import jax
import jax.numpy as jnp
from jax import lax
from jax.experimental import pallas as pl
from jax.experimental.pallas import tpu as pltpu
from jax.sharding import PartitionSpec as P

F32 = jnp.float32
BF16 = jnp.bfloat16
I32 = jnp.int32
HIGHEST = lax.Precision.HIGHEST

PIX = 625
LANES = 128
CHUNKS = 5
PADPIX = CHUNKS * LANES
TILES = 64
REPS = 4
SLOTS = 1024
BASIS = 10
QUAD = 4
CCD = 4
GROUP = 16
GROUPS = TILES // GROUP
GSLOTS = GROUP * 16
ROWS = 48
GK = GROUP * ROWS
ORDER = 256
HALF = 128
TERMS = 16
UNROLL = 2
PAIRS = [(q, r) for q in range(QUAD) for r in range(q, QUAD)]
MESH = pl.DeviceIdType.MESH
VMEM = pl.BlockSpec(memory_space=pltpu.VMEM)


def iota(shape, axis):
    return lax.broadcasted_iota(I32, shape, axis)


def flat(ref):
    return jnp.concatenate([ref[i : i + 1, :].astype(F32) for i in range(8)], axis=1)


def pack_meta(cf_ref, iv_ref, cd_ref, out_ref):
    meta = jnp.concatenate(
        [cf_ref[k].astype(F32) for k in range(BASIS)]
        + [flat(iv_ref), flat(cd_ref), jnp.zeros((LANES - QUAD * BASIS - 2, SLOTS), F32)],
        axis=0,
    )
    rows = jnp.transpose(meta).reshape(TILES, 16, LANES)
    left = rows[:, :8].reshape(TILES * 8, LANES)
    right = rows[:, 8:].reshape(TILES * 8, LANES)
    out_ref[...] = (left + pltpu.roll(right, 64, 1)).reshape(TILES, 8, LANES).astype(BF16)


def unpack_meta(got_ref):
    rows = got_ref[...].astype(F32)
    other = pltpu.roll(rows.reshape(TILES * 8, LANES), 64, 1).reshape(TILES, 8, LANES)
    return jnp.transpose(jnp.concatenate([rows, other], axis=1).reshape(SLOTS, LANES))


def pack_block(st_ref, chunk, out_ref):
    if chunk < CHUNKS - 1:
        block = st_ref[chunk * LANES : (chunk + 1) * LANES, :].astype(F32)
    else:
        body = st_ref[chunk * LANES : PIX - 1, :].astype(F32)
        last = jnp.broadcast_to(st_ref[PIX - 1 : PIX, :].astype(F32), (16, SLOTS))
        row = iota((16, SLOTS), 0)
        tail = jnp.where(row == 0, last, jnp.where(row == 1, 1.0, 0.0))
        block = jnp.concatenate([body, tail], axis=0)
    out_ref[chunk] = jnp.transpose(block).astype(BF16).reshape(TILES, 16, LANES)


def fill_key(counts_ref, src_ref, key_ref):
    owner = (iota((TILES, SLOTS), 0) == iota((TILES, SLOTS), 1) // 16).astype(F32).astype(BF16)
    count = jnp.concatenate(
        [counts_ref[...].astype(F32), jnp.zeros((12, TILES), F32)], axis=0
    ).astype(BF16)
    laid = jnp.dot(count, owner, preferred_element_type=F32)
    lane = iota((1, SLOTS), 1)
    blob = (lane // 4) % 4
    mine = jnp.zeros((1, SLOTS), F32)
    for b in range(REPS):
        mine = jnp.where(blob == b, laid[b : b + 1, :], mine)
    live = (lane % 4).astype(F32) < mine
    key_ref[...] = jnp.where(live, src_ref[0:1, :] + blob * ORDER, -1)


def fill_move(move_ref):
    row = iota((SLOTS, 1), 0)
    home = ((row // 4) % 4) * ORDER + (row // 16) * 4 + row % 4
    move_ref[...] = (home == iota((SLOTS, SLOTS), 1)).astype(F32).astype(BF16)


def fill_hot(key_ref, hot_ref):
    hot_ref[...] = (iota((SLOTS, SLOTS), 0) == key_ref[...]).astype(F32).astype(BF16)


def fill_select(meta, select_ref):
    cols = meta.astype(BF16)
    image = iota((ROWS, 1), 0)
    own_ccd = jnp.where(image < CCD * BASIS, image % CCD, -1).astype(F32)
    hit = own_ccd == meta[QUAD * BASIS + 1 : QUAD * BASIS + 2, :]
    owner = iota((16, GSLOTS), 1) // 16
    laid = []
    for q in range(QUAD):
        spread = (iota((ROWS, LANES), 1) == (image // CCD) * QUAD + q).astype(F32).astype(BF16)
        value = jnp.dot(spread, cols, preferred_element_type=F32)
        laid.append(jnp.where(hit, value, 0.0).astype(BF16))
    for t in range(GROUP):
        seen = (owner == t).astype(F32).astype(BF16)
        for h in range(GROUPS):
            for q in range(QUAD):
                for part in range(ROWS // 16):
                    select_ref[
                        h,
                        t * ROWS + part * 16 : t * ROWS + (part + 1) * 16,
                        q * GSLOTS : (q + 1) * GSLOTS,
                    ] = seen * laid[q][part * 16 : (part + 1) * 16, h * GSLOTS : (h + 1) * GSLOTS]


def render(h, every_ref, select_ref, model_ref):
    image = lax.dot_general(
        every_ref[pl.ds(h * 8, 8)].reshape(GK, PADPIX),
        select_ref[h],
        (((0,), (0,)), ((), ())),
        preferred_element_type=F32,
    )
    at = pl.ds(pl.multiple_of(h * GSLOTS, GSLOTS), GSLOTS)
    for q in range(QUAD):
        model_ref[q, :, at] = image[:, q * GSLOTS : (q + 1) * GSLOTS].astype(BF16)


def accumulate(chunk, xt_ref, own_ref, model_ref, scale_ref, term_ref, rows=16):
    for lane in range(SLOTS // LANES):
        at = slice(lane * LANES, (lane + 1) * LANES)
        quarter = jnp.broadcast_to(scale_ref[0:1, at], (rows, LANES))
        live = jnp.broadcast_to(scale_ref[1:2, at], (rows, LANES))

        def step(i, sums):
            here = pl.ds(pl.multiple_of(i * rows, rows), rows)
            there = pl.ds(pl.multiple_of(chunk * LANES + i * rows, rows), rows)
            x = xt_ref[there, at].astype(F32)
            gap = x - own_ref[here, at]
            weight = live / (1.0 + quarter * (gap * gap))
            m = [model_ref[q, there, at].astype(F32) for q in range(QUAD)]
            wm = [weight * v for v in m]
            new = [wm[q] * m[r] for q, r in PAIRS] + [wm[q] * x for q in range(QUAD)]
            return tuple(s + (v[0:8] + v[8:16]) for s, v in zip(sums, new))

        sums = lax.fori_loop(
            0,
            LANES // rows,
            step,
            tuple(jnp.zeros((8, LANES), F32) for _ in range(14)),
            unroll=UNROLL,
        )
        for n, s in enumerate(sums):
            term_ref[n, :, at] += s


def finish_terms(term_ref, move_ref):
    rows = [jnp.sum(term_ref[n], axis=0, keepdims=True) for n in range(14)]
    block = jnp.concatenate(rows + [jnp.zeros((TERMS - 14, SLOTS), F32)], axis=0)
    moved = jnp.dot(
        jnp.concatenate(halves(block), axis=0), move_ref[...], preferred_element_type=F32
    )
    return moved[0:TERMS] + moved[TERMS : 2 * TERMS] + moved[2 * TERMS : 3 * TERMS]


def invert(mat_ref, zero_ref):
    lane = iota((8, LANES), 1)
    sub = iota((8, LANES), 0)
    zero = zero_ref[...]

    def spread(v, j):
        return jnp.broadcast_to(v[j : j + 1, :], (8, LANES))

    def block(o, _):
        top = pl.multiple_of(o * 32, 32)
        rows = [mat_ref[pl.ds(top + 8 * m, 8), :] for m in range(4)]
        for kb in range(4):
            base = 8 * kb
            panel = rows[kb]
            cols = [
                jnp.broadcast_to(panel[:, base + k : base + k + 1], (8, LANES)) + zero
                for k in range(8)
            ]
            for j in range(8):
                factor = cols[j]
                pivot = 1.0 / spread(factor, j)
                row = jnp.where(lane == base + j, 1.0, spread(panel, j)) * pivot
                kept = jnp.where(lane == base + j, 0.0, panel)
                panel = jnp.where(sub == j, row, kept - factor * row)
                for k in range(j + 1, 8):
                    side = spread(cols[k], j) * pivot
                    cols[k] = jnp.where(sub == j, side, cols[k] - factor * side)
            spreads = [spread(panel, j) for j in range(8)]
            rows[kb] = panel
            for m in range(4):
                if m == kb:
                    continue
                old = rows[m]
                new = jnp.where((lane >= base) & (lane < base + 8), 0.0, old)
                even = zero
                for j in range(0, 8, 2):
                    a = jnp.broadcast_to(old[:, base + j : base + j + 1], (8, LANES))
                    b = jnp.broadcast_to(old[:, base + j + 1 : base + j + 2], (8, LANES))
                    new = new - a * spreads[j]
                    even = even + b * spreads[j + 1]
                rows[m] = new - even
        whole = mat_ref[...]
        done = jnp.concatenate(rows, axis=0)
        kept = jnp.where(iota((HALF, LANES), 1) < 32, 0.0, whole)
        mat_ref[...] = pltpu.roll(kept - full(whole[:, 0:32], done), LANES - 32, 1)
        mat_ref[pl.ds(top, 32), :] = pltpu.roll(done, LANES - 32, 1)
        return 0

    lax.fori_loop(0, 4, block, 0)


def full(a, b):
    return jnp.dot(a, b, preferred_element_type=F32, precision=HIGHEST)


def fill_home(source, home_ref):
    where = iota((ORDER, SLOTS), 0)
    for q in range(QUAD):
        home_ref[q] = (where == source[q : q + 1, :]).astype(F32).astype(BF16)


def halves(v):
    high = v.astype(BF16)
    rest = v - high.astype(F32)
    mid = rest.astype(BF16)
    return high, mid, (rest - mid.astype(F32)).astype(BF16)


def solve(terms, home_ref, side_ref, work_ref, zero_ref):
    gram = jnp.zeros((ORDER, ORDER), F32)
    row = jnp.zeros((8, ORDER), F32)
    for r in range(QUAD):
        for part in range(2):
            mixed = None
            for q in range(r + 1):
                value = terms[PAIRS.index((q, r)) : PAIRS.index((q, r)) + 1, :]
                value = halves(value * (0.5 if q == r else 1.0))[part]
                step = home_ref[q] * value
                mixed = step if mixed is None else mixed + step
            side_ref[part * ORDER : (part + 1) * ORDER, :] = mixed
        one, two, three = halves(terms[10 + r : 11 + r, :])
        side_ref[2 * ORDER : 2 * ORDER + 16, :] = jnp.concatenate(
            [one.astype(F32), two.astype(F32), three.astype(F32), jnp.zeros((13, SLOTS), F32)], axis=0
        ).astype(BF16)
        got = lax.dot_general(
            side_ref[...], home_ref[r], (((1,), (1,)), ((), ())), preferred_element_type=F32
        )
        gram = gram + (got[:ORDER] + got[ORDER : 2 * ORDER])
        row = row + got[2 * ORDER : 2 * ORDER + 8]
    row = row[0:1] + row[1:2] + row[2:3]
    eye = iota((HALF, HALF), 0) == iota((HALF, HALF), 1)
    one = jnp.where(eye, 1.0, 0.0)

    def turn(v):
        return jnp.transpose(jnp.broadcast_to(v, (HALF, HALF)))

    a11 = gram[:HALF, :HALF]
    a22 = gram[HALF:, HALF:]
    a12 = gram[:HALF, HALF:] + jnp.transpose(gram[HALF:, :HALF])
    a21 = jnp.transpose(a12)
    r1_row, r2_row = row[:, :HALF], row[:, HALF:]
    r1_col, r2_col = turn(r1_row)[:, 0:1], turn(r2_row)[:, 0:1]
    work_ref[...] = a11 + jnp.transpose(a11) + one
    invert(work_ref, zero_ref)
    top = work_ref[...]
    tie = full(a21, top)
    work_ref[...] = a22 + jnp.transpose(a22) + one - full(tie, a12)
    invert(work_ref, zero_ref)
    low = work_ref[...]
    v = r2_col - jnp.sum(tie * r1_row, axis=1, keepdims=True)
    f2_row = jnp.sum(low * v, axis=0, keepdims=True)
    f2_col = jnp.sum(low * turn(v)[0:1, :], axis=1, keepdims=True)
    f1_row = jnp.sum(top * r1_col, axis=0, keepdims=True) - jnp.sum(tie * f2_col, axis=0, keepdims=True)
    d2 = jnp.sum(jnp.where(eye, low, 0.0), axis=0, keepdims=True)
    d1 = jnp.sum(jnp.where(eye, top, 0.0), axis=0, keepdims=True) + jnp.sum(
        full(low, tie) * tie, axis=0, keepdims=True
    )
    return f1_row / jnp.sqrt(d1), f2_row / jnp.sqrt(d2)


def remote(src, dst, send, recv, **where):
    return pltpu.make_async_remote_copy(
        src_ref=src, dst_ref=dst, send_sem=send, recv_sem=recv, device_id=where, device_id_type=MESH
    )


def whole_kernel(
    st_ref, cf_ref, iv_ref, cd_ref, src_ref, counts_ref, bases_ref, out_ref,
    mine_ref, key_ref, move_ref, meta_out, meta_in, src_out, src_in, home_ref, side_ref, zero_ref,
    packed, got, every, xt_ref, hot_ref, select_ref, model_ref, scale_ref, own_ref, term_ref,
    tables, parts, mean_own, means, count_ref, terms_out, terms_in, work_ref,
    a_send, a_recv, b_send, b_recv, t_send, t_recv, m_send, m_recv, e_send, e_recv, s_send, s_recv,
):
    me = lax.axis_index("tile")
    g = lax.axis_index("rep")
    x, z, c = me // 16, (me // 2) % 8, me % 2

    def peer(dx, dz, core):
        return (((x + dx + 4) % 4) * 8 + (z + dz + 8) % 8) * 2 + core

    barrier = pltpu.get_barrier_semaphore()

    def greet(o, _):
        pl.semaphore_signal(barrier, inc=1, device_id={"tile": (me + o) % TILES}, device_id_type=MESH)
        return 0

    lax.fori_loop(1, TILES, greet, 0)
    for d in range(1, REPS):
        pl.semaphore_signal(barrier, inc=1, device_id={"rep": (g + d) % REPS}, device_id_type=MESH)

    def send_all(src, dst, n):
        def one(o, _):
            p = (me + o) % TILES
            remote(src.at[p], dst.at[me], a_send.at[n], a_recv.at[n], tile=p).start()
            return 0

        lax.fori_loop(1, TILES, one, 0)
        dst[pl.ds(me, 1)] = src[pl.ds(me, 1)]

    def all_done(src, dst, n):
        many = pl.ds(0, TILES - 1)
        return remote(src.at[many], dst.at[many], a_send.at[n], a_recv.at[n], tile=peer(0, 1, c))

    def send_block(n):
        send_all(packed.at[n], got.at[n], n)

    def block_done(n):
        return all_done(packed.at[n], got.at[n], n)

    def blocks_done(stage, count):
        many = every.at[pl.ds(0, count), 0]
        return remote(many, many, b_send.at[stage], b_recv.at[stage], tile=peer(0, 1, c))

    def send_bases(stage, ref, dx, dz, core):
        remote(ref, ref, b_send.at[stage], b_recv.at[stage], tile=peer(dx, dz, core)).start()

    here = x * 8 + z

    def origin(dx, dz):
        return every.at[((x + dx + 4) % 4) * 8 + (z + dz + 8) % 8, c]

    def stage_z1():
        for dz in (1, -1, 2, -2):
            remote(
                mine_ref, every.at[here, c], b_send.at[0], b_recv.at[0], tile=peer(0, dz, c)
            ).start()

    def stage_z2():
        send_bases(1, origin(0, -2), 0, 1, c)
        send_bases(1, origin(0, 2), 0, -1, c)
        send_bases(1, origin(0, -2), 0, 2, c)

    def stage_x1(stage, offsets):
        for dz in offsets:
            for dx in (1, -1):
                send_bases(stage, origin(0, dz), dx, 0, c)

    def stage_x2(stage, ahead, back):
        for dz in ahead:
            send_bases(stage, origin(-1, dz), 1, 0, c)
        for dz in back:
            send_bases(stage, origin(1, dz), -1, 0, c)

    def column(shift):
        return pl.ds(((x + shift) % 4) * 8, 8)

    def stage_core1():
        send_bases(4, every.at[column(0), c], 0, 0, 1 - c)

    def stage_core2():
        send_bases(5, every.at[column(1), c], 0, 0, 1 - c)
        send_bases(5, every.at[column(3), c], 0, 0, 1 - c)

    def stage_core3():
        blocks_done(3, 5).wait_recv()
        blocks_done(8, 3).wait_recv()
        send_bases(6, every.at[column(2), c], 0, 0, 1 - c)

    def show(shift):
        render((x + shift) % 4, every, select_ref, model_ref)

    def stack(n):
        block_done(n).wait_recv()
        turned = jnp.transpose(got[n].reshape(SLOTS, LANES).astype(F32)).astype(BF16)
        xt_ref[n * LANES : (n + 1) * LANES, :] = turned
        part = lax.dot_general(
            turned, hot_ref[...], (((1,), (1,)), ((), ())), preferred_element_type=F32
        )
        for b in range(REPS):
            tables[n, b] = part[:, b * ORDER : (b + 1) * ORDER].astype(BF16)
        for d in range(1, REPS):
            b = (g + d) % REPS
            remote(tables.at[n, b], parts.at[n, g], t_send.at[n], t_recv.at[n], rep=b).start()
        parts[n, pl.ds(g, 1)] = tables[n, pl.ds(g, 1)]

    def three(src, dst, send, recv, n):
        many = pl.ds(0, REPS - 1)
        return remote(src.at[n, many], dst.at[n, many], send.at[n], recv.at[n], rep=(g + 1) % REPS)

    def mean(n):
        three(tables, parts, t_send, t_recv, n).wait_recv()
        total = parts[n, 0].astype(F32)
        for other in range(1, REPS):
            total = total + parts[n, other].astype(F32)
        if n == CHUNKS - 1:
            at = PIX - (CHUNKS - 1) * LANES
            count_ref[...] = jnp.broadcast_to(total[at : at + 1, :], (8, ORDER))
        value = (total / (1.0 + count_ref[0:1, :])).astype(BF16)
        mean_own[n, 0] = value
        for d in range(1, REPS):
            remote(
                mean_own.at[n, 0], means.at[n, g], m_send.at[n], m_recv.at[n], rep=(g + d) % REPS
            ).start()
        means[n, pl.ds(g, 1)] = mean_own[n]

    def terms(n):
        three(means, means, m_send, m_recv, n).wait_recv()
        joined = jnp.concatenate([means[n, b] for b in range(REPS)], axis=1)
        own_ref[...] = jnp.dot(joined, hot_ref[...], preferred_element_type=F32)
        accumulate(n, xt_ref, own_ref, model_ref, scale_ref, term_ref)

    pack_meta(cf_ref, iv_ref, cd_ref, meta_out)
    pack_block(st_ref, 4, packed)
    mine_ref[...] = jnp.zeros_like(mine_ref)
    mine_ref[0 : CCD * BASIS, 0:PIX] = jnp.concatenate(
        [bases_ref[k].astype(F32) for k in range(BASIS)], axis=0
    ).astype(BF16)
    pl.semaphore_wait(barrier, TILES - 1 + REPS - 1)
    stage_z1()
    every[pl.ds(here, 1), pl.ds(c, 1)] = mine_ref[...].reshape(1, 1, ROWS, PADPIX)
    pack_block(st_ref, 0, packed)
    fill_key(counts_ref, src_ref, key_ref)
    fill_hot(key_ref, hot_ref)
    blocks_done(0, 4).wait_recv()
    stage_z2()
    stage_x1(2, (0, 1, -1, 2, -2))
    send_all(meta_out, meta_in, CHUNKS)
    send_block(4)
    pack_block(st_ref, 1, packed)
    fill_move(move_ref)
    wide = jnp.concatenate([src_ref[...].astype(F32), jnp.zeros((12, SLOTS), F32)], axis=0)
    wide = jnp.dot(wide.astype(BF16), move_ref[...], preferred_element_type=F32)
    for b in range(REPS):
        src_out[0, b] = wide[0:8, b * ORDER : (b + 1) * ORDER]
    for d in range(1, REPS):
        b = (g + d) % REPS
        remote(src_out.at[0, b], src_in.at[0, g], s_send.at[0], s_recv.at[0], rep=b).start()
    src_in[0, pl.ds(g, 1)] = src_out[0, pl.ds(g, 1)]
    blocks_done(1, 3).wait_recv()
    stage_x1(7, (3, 4, -3))
    stage_core1()
    send_block(0)
    pack_block(st_ref, 2, packed)
    pack_block(st_ref, 3, packed)
    send_block(1)
    term_ref[...] = jnp.zeros_like(term_ref)
    zero_ref[...] = jnp.zeros_like(zero_ref)
    all_done(meta_out, meta_in, CHUNKS).wait_recv()
    meta = unpack_meta(meta_in)
    ivar = meta[QUAD * BASIS : QUAD * BASIS + 1, :]
    scale_ref[0:1, :] = ivar * 0.25
    scale_ref[1:2, :] = jnp.where(key_ref[...] >= 0, ivar, 0.0)
    fill_select(meta, select_ref)
    blocks_done(2, 10).wait_recv()
    stage_x2(3, (0, 1, 2), (-1, -2))
    blocks_done(7, 6).wait_recv()
    stage_x2(8, (3, 4), (-3,))
    stage_core2()
    send_block(2)
    send_block(3)
    three(src_out, src_in, s_send, s_recv, 0).wait_recv()
    fill_home(
        jnp.concatenate([src_in[0, k] for k in range(REPS)], axis=1).astype(I32), home_ref
    )
    blocks_done(4, 8).wait_recv()
    show(0)
    stack(4)
    stack(0)
    mean(4)
    blocks_done(5, 16).wait_recv()
    show(1)
    show(3)
    stack(1)
    mean(0)
    stage_core3()
    stack(2)
    mean(1)
    blocks_done(6, 8).wait_recv()
    show(2)
    terms(4)
    stack(3)
    mean(2)
    terms(0)
    terms(1)
    mean(3)
    terms(2)
    terms(3)
    block = finish_terms(term_ref, move_ref)
    for b in range(REPS):
        terms_out[0, b] = block[:, b * ORDER : (b + 1) * ORDER]
    for d in range(1, REPS):
        b = (g + d) % REPS
        remote(terms_out.at[0, b], terms_in.at[0, g], e_send.at[0], e_recv.at[0], rep=b).start()
    terms_in[0, pl.ds(g, 1)] = terms_out[0, pl.ds(g, 1)]
    three(terms_out, terms_in, e_send, e_recv, 0).wait_recv()
    joined = jnp.concatenate([terms_in[0, k] for k in range(REPS)], axis=1)
    left, right = solve(joined, home_ref, side_ref, work_ref, zero_ref)
    out_ref[:, :HALF] = left
    out_ref[:, HALF:] = right

    for n in range(CHUNKS):
        block_done(n).wait_send()
    all_done(meta_out, meta_in, CHUNKS).wait_send()
    three(src_out, src_in, s_send, s_recv, 0).wait_send()
    for stage, count in enumerate((4, 3, 10, 5, 8, 16, 8, 6, 3)):
        blocks_done(stage, count).wait_send()
    for n in range(CHUNKS):
        three(tables, parts, t_send, t_recv, n).wait_send()
        three(means, means, m_send, m_recv, n).wait_send()
    three(terms_out, terms_in, e_send, e_recv, 0).wait_send()


def struct(shape, dtype):
    return jax.ShapeDtypeStruct(shape, dtype)


def local(stamps, coefs, ivar, ccd, bases, sources, counts):
    dma = pltpu.SemaphoreType.DMA
    return pl.pallas_call(
        whole_kernel,
        out_shape=struct((1, ORDER), F32),
        in_specs=[VMEM] * 7,
        out_specs=VMEM,
        scratch_shapes=[
            pltpu.VMEM((ROWS, PADPIX), BF16),
            pltpu.VMEM((1, SLOTS), I32),
            pltpu.VMEM((SLOTS, SLOTS), BF16),
            pltpu.VMEM((TILES, 8, LANES), BF16),
            pltpu.VMEM((TILES, 8, LANES), BF16),
            pltpu.VMEM((1, REPS, 8, ORDER), F32),
            pltpu.VMEM((1, REPS, 8, ORDER), F32),
            pltpu.VMEM((QUAD, ORDER, SLOTS), BF16),
            pltpu.VMEM((2 * ORDER + 16, SLOTS), BF16),
            pltpu.VMEM((8, LANES), F32),
            pltpu.VMEM((CHUNKS, TILES, 16, LANES), BF16),
            pltpu.VMEM((CHUNKS, TILES, 16, LANES), BF16),
            pltpu.VMEM((32, 2, ROWS, PADPIX), BF16),
            pltpu.VMEM((PADPIX, SLOTS), BF16),
            pltpu.VMEM((SLOTS, SLOTS), BF16),
            pltpu.VMEM((GROUPS, GK, QUAD * GSLOTS), BF16),
            pltpu.VMEM((QUAD, PADPIX, SLOTS), BF16),
            pltpu.VMEM((8, SLOTS), F32),
            pltpu.VMEM((LANES, SLOTS), F32),
            pltpu.VMEM((14, 8, SLOTS), F32),
            pltpu.VMEM((CHUNKS, REPS, LANES, ORDER), BF16),
            pltpu.VMEM((CHUNKS, REPS, LANES, ORDER), BF16),
            pltpu.VMEM((CHUNKS, 1, LANES, ORDER), BF16),
            pltpu.VMEM((CHUNKS, REPS, LANES, ORDER), BF16),
            pltpu.VMEM((8, ORDER), F32),
            pltpu.VMEM((1, REPS, TERMS, ORDER), F32),
            pltpu.VMEM((1, REPS, TERMS, ORDER), F32),
            pltpu.VMEM((HALF, HALF), F32),
            dma((CHUNKS + 1,)),
            dma((CHUNKS + 1,)),
            dma((9,)),
            dma((9,)),
            dma((CHUNKS,)),
            dma((CHUNKS,)),
            dma((CHUNKS,)),
            dma((CHUNKS,)),
            dma((1,)),
            dma((1,)),
            dma((1,)),
            dma((1,)),
        ],
        compiler_params=pltpu.CompilerParams(
            collective_id=0, has_side_effects=True, vmem_limit_bytes=60 * 1024 * 1024
        ),
    )(
        stamps,
        jnp.transpose(coefs, (1, 0, 2)),
        ivar.reshape(8, LANES),
        ccd.reshape(8, LANES),
        sources,
        jnp.transpose(counts),
        jnp.transpose(bases, (1, 0, 2)),
    )


def solution(mesh):
    return jax.shard_map(
        local,
        mesh=mesh,
        in_specs=(
            P(None, ("tile", "rep")),
            P(None, None, ("tile", "rep")),
            P(("tile", "rep")),
            P(("tile", "rep")),
            P(("tile", "rep"), None, None),
            P(None, ("tile", "rep")),
            P(("tile", "rep"), None),
        ),
        out_specs=P(("tile", "rep"), None),
        check_vma=False,
    )
```
